32 devices in a mesh: dom: 16 (over z, x, core), cell: 2 (over y).
Axes of the slice: x: 2, y: 2, z: 4, core: 2. Of those that a mesh axis runs over, the one named last changes fastest.
Arguments:
- models: bfloat16 [2, 512, 4096], P(None, 'dom', 'cell'), may hold values from -12 to 12
- gradients: bfloat16 [2, 512, 4096], P(None, 'dom', 'cell'), may hold values from -48 to 48
- length_scale: float32 [1], replicated, may hold values from 3 to 12
Outputs:
- update: float32 [2, 512, 4096], P(None, 'dom', 'cell')
The draws below stay inside these ranges and needn't reach their ends.
All inputs are finite; a program needn't handle non-finite values.
Results may differ from the reference program's by a relative error of at most 0.00045.
The reference program's roundings to bfloat16 on the way (of `kernel`) count: a program that leaves them out, or rounds other values in their place, can miss the bound.
Values may be sent and summed in bfloat16 or wider, within the bound.
A program may use at most 64 MiB of HBM per device.

```python
import math
import jax
import jax.numpy as jnp

P_SIZE = 512
NC = 4096


def draw_models(key, part):
    first, second, third = jax.random.split(key, 3)
    latent = jax.random.normal(first, (P_SIZE, 8), jnp.float32)
    basis_fields = jax.random.normal(second, (2, 8, NC), jnp.float32)
    jitter = 0.7 * jax.random.normal(third, (2, P_SIZE, NC), jnp.float32)
    fields = jnp.einsum('pk,jkc->jpc', latent, basis_fields) / math.sqrt(8.0) + jitter
    return jnp.clip(fields, -12.0, 12.0).astype(jnp.bfloat16)


def block_levels(stream_key, shape, pieces, smallest, largest):
    level = 1.0
    for position, shards_of in pieces:
        draws = jax.random.uniform(jax.random.fold_in(jax.random.fold_in(stream_key, 6), position), (shards_of,), jnp.float32, smallest / len(pieces), largest / len(pieces))
        level = level * jnp.repeat(jnp.exp(draws), shape[position] // shards_of).reshape((-1,) + (1,) * (len(shape) - 1 - position))
    return level


def scatter_about(rng, extent, spread, reach, pieces=(), kind=jnp.bfloat16):
    values = jax.random.normal(rng, extent, jnp.float32) * spread
    if len(pieces) > 0:
        values = block_levels(rng, extent, pieces, -0.22, 0.18) * values
    return jnp.clip(values, min=-reach, max=reach).astype(kind)


def setup_inputs(seed: int = 0) -> dict:
    key_of = jax.random.split(jax.random.key(seed), 4)
    return {
        "models": draw_models(jax.random.fold_in(key_of[3], 71), 0),
        "gradients": scatter_about(key_of[1], (2, P_SIZE, NC), 8.0, 48.0, ((1, 16), (2, 2))),
        "length_scale": jnp.clip(jnp.exp(jax.random.uniform(key_of[2], (1,), jnp.float32, math.log(3.0), math.log(12.0))), 3.0, 12.0),
    }


def reference(models, gradients, length_scale):
    scale_value = length_scale[0]
    wide_models = models.astype(jnp.float32)
    gram_sum = jnp.einsum("kpc,kqc->pq", wide_models, wide_models)
    squares = jnp.diagonal(gram_sum)
    distance = squares[:, None] + squares[None, :] - 2.0 * gram_sum
    kernel = jnp.exp(-distance / (scale_value * NC)).astype(jnp.bfloat16)
    wide_kernel = kernel.astype(jnp.float32)
    rowsum = jnp.sum(wide_kernel, axis=1)
    attract = jnp.einsum("pq,kqc->kpc", wide_kernel, gradients.astype(jnp.float32))
    pulled = jnp.einsum("pq,kqc->kpc", wide_kernel, wide_models)
    update = (attract + (2.0 / scale_value) * (rowsum[None, :, None] * wide_models - pulled)) / P_SIZE
    return update
```

```python
import functools
import math

import jax
import jax.numpy as jnp
from jax import lax
from jax.experimental import pallas as pl
from jax.experimental.pallas import tpu as pltpu
from jax.sharding import PartitionSpec as P

MESH = pl.DeviceIdType.MESH


def plain_body(models, gradients, length_scale):
    local_models, local_grads = (
        lax.all_to_all(models, "dom", split_axis=2, concat_axis=1, tiled=True),
        lax.all_to_all(gradients, "dom", split_axis=2, concat_axis=1, tiled=True),
    )
    cell_block = local_models.shape[2]
    particles = local_models.shape[1]
    cell_count = cell_block * lax.axis_size("dom") * lax.axis_size("cell")
    scale_value = length_scale[0]
    divisor = scale_value * cell_count
    partial_value = jnp.einsum(
        "kpc,kqc->pq", local_models, local_models, preferred_element_type=jnp.float32
    )
    summed = lax.psum(partial_value, "cell")
    row_block = lax.psum_scatter(summed, "dom", scatter_dimension=0, tiled=True)
    row_count = row_block.shape[0]
    row_start = lax.axis_index("dom") * row_count
    own_squares = jnp.diagonal(lax.dynamic_slice_in_dim(row_block, row_start, row_count, 1))
    squares = lax.all_gather(own_squares, "dom", axis=0, tiled=True)
    distance = own_squares[:, None] + squares[None, :] - 2.0 * row_block
    kernel = lax.all_gather(
        jnp.exp(-distance / divisor).astype(jnp.bfloat16), "dom", axis=0, tiled=True
    )
    rowsum = jnp.sum(kernel.astype(jnp.float32), axis=1)
    stacked = jnp.concatenate((local_grads, local_models), axis=2)
    product = jnp.einsum("pq,kqc->kpc", kernel, stacked, preferred_element_type=jnp.float32)
    attract = product[:, :, :cell_block]
    pulled = product[:, :, cell_block:]
    update = (
        attract
        + 2.0 / scale_value * (rowsum[None, :, None] * local_models.astype(jnp.float32) - pulled)
    ) / particles
    return lax.all_to_all(update, "dom", split_axis=1, concat_axis=2, tiled=True)


LIFT = 512.0


def stein_kernel(
    layers, group, planes,
    scale_ref, models_ref, grads_ref, out_ref, factor_ref,
    m_loc, g_loc, code, mbuf, hbuf, high, low, part, inbox, swap_out, swap_in, base,
    krow, kin, kin_wide, kin_tall, kfull, outbox,
    loc_sem, m_send, m_recv, f_send, f_recv, a_send, a_recv, z_send, z_recv,
    rs_send, rs_recv, s_sem, k_send, k_recv, o_send, o_recv,
):
    fields, rows, width = models_ref.shape
    cells = width // group
    half = cells // 2
    slab = group * rows
    count = layers * slab
    chips = group // 2 * planes
    peers = group * planes
    strip = slab // chips
    chunks = fields * 2
    pair = 2 * slab
    total_cells = width * planes
    dom = lax.axis_index("dom")
    y = lax.axis_index("cell")
    z = dom // group
    g = dom % group
    core = g % 2
    chip = g // 2 * planes + y
    near = z // 2
    far = 1 - near
    inner = jnp.logical_and(z > 0, z < layers - 1)
    is_end = jnp.logical_not(inner)
    mate = layers - 1 - z
    tip = near * (layers - 1)
    far_tip = far * (layers - 1)
    toward = jnp.where(inner, mate, 1 + near)
    even = core == 0
    odd = core == 1

    def both(left, right):
        return jnp.logical_and(left, right)

    def at(layer, which):
        return (layer * group + which, y)

    def at_chip(layer, which, kind):
        return (layer * group + which // planes * 2 + kind, which % planes)

    def ring(k):
        return (g + k) % group

    def back(k):
        return (g + group - k) % group

    def remote(src, dst, send, recv, device):
        return pltpu.make_async_remote_copy(
            src_ref=src, dst_ref=dst, send_sem=send, recv_sem=recv,
            device_id=device, device_id_type=MESH,
        )

    loads = [
        pltpu.make_async_copy(models_ref, m_loc, loc_sem.at[0]),
        pltpu.make_async_copy(grads_ref, g_loc, loc_sem.at[1]),
    ]
    for copy in loads:
        copy.start()

    barrier = pltpu.get_barrier_semaphore()
    me = dom * planes + y
    everyone = layers * peers

    def greet(k, carry):
        other = (me + k) % everyone
        pl.semaphore_signal(
            barrier, inc=1, device_id=(other // planes, other % planes), device_id_type=MESH
        )
        return carry

    lax.fori_loop(1, everyone, greet, 0)
    pl.semaphore_wait(barrier, everyone - 1)

    def m_part(side, to):
        return models_ref.at[:, :, pl.ds(pl.multiple_of(to * cells + side * half, 128), half)]

    def m_copy(slot, side, k):
        to = ring(k)
        return remote(
            m_part(side, to), mbuf.at[to % 2, z, g],
            m_send.at[slot, k], m_recv.at[z, g], at(1 + side, to),
        )

    def m_own():
        return pltpu.make_async_copy(m_part(near, g), mbuf.at[core, z, g], loc_sem.at[2])

    for slot, side in ((0, far), (1, near)):
        for k in range(group):
            if slot == 1 and k == 0:
                @pl.when(inner)
                def _():
                    m_own().start()

                @pl.when(is_end)
                def _():
                    m_copy(1, near, 0).start()
            else:
                m_copy(slot, side, k).start()

    for copy in loads:
        copy.wait()

    scale = scale_ref[0]

    def a_copy(s, k):
        to = ring(k)
        return remote(
            code.at[s, to], hbuf.at[s, z, g], a_send.at[s, k], a_recv.at[s, g], at(z, to)
        )

    weight = 2.0 * LIFT / jnp.full((rows, half), scale, jnp.float32)
    for s in range(chunks):
        field, side = s // 2, s % 2
        for to in range(group):
            span = slice(to * cells + side * half, to * cells + side * half + half)
            value = g_loc[field, :, span].astype(jnp.float32) * LIFT
            value = value - weight * m_loc[field, :, span].astype(jnp.float32)
            square = value * value
            code[s, to] = (square * square * square * value * jnp.abs(value)).astype(jnp.bfloat16)
        for k in range(1, group):
            a_copy(s, k).start()
        hbuf[s, z, g] = code[s, g]

    def z_copy(s, layer, outward):
        block = hbuf.at[s, layer]
        return remote(
            block, block, z_send.at[outward, s, layer], z_recv.at[s, layer],
            at(tip if outward else toward, g),
        )

    def decode(s, layer):
        value = hbuf[s, layer].reshape(slab, half).astype(jnp.float32)
        root = jnp.exp2(jnp.log2(jnp.abs(value)) * 0.125)
        root = jnp.where(value < 0.0, -root, root)
        upper = root.astype(jnp.bfloat16)
        high[s, layer] = upper
        low[s, layer] = (root - upper.astype(jnp.float32)).astype(jnp.bfloat16)

    def own_ready(s):
        for k in range(1, group):
            source = back(k)
            remote(
                code.at[s, g], hbuf.at[s, z, source], a_send.at[s, k], a_recv.at[s, source],
                at(z, source),
            ).wait_recv()

    def own_go(s):
        own_ready(s)
        z_copy(s, z, 0).start()

        @pl.when(inner)
        def _():
            z_copy(s, z, 1).start()

    def pass_on(s, layer, outward):
        z_copy(s, layer, outward).wait_recv()
        z_copy(s, layer, outward).start()

    def f_copy(kind, layer):
        block = mbuf.at[kind, layer]
        return remote(
            block, block, f_send.at[layer], f_recv.at[layer], at(z, g + 1 - 2 * core)
        )

    def m_wait(layer, own):
        for k in range(1 if own else 0, group):
            source = back(k)
            remote(
                m_part(near, g), mbuf.at[core, layer, source], m_send.at[0, k],
                m_recv.at[layer, source], at(z, source),
            ).wait_recv()
        if own:
            m_own().wait()
        f_copy(core, layer).start()

    contract = (((1,), (1,)), ((), ()))

    def inner_product(left, right):
        return lax.dot_general(left, right, contract, preferred_element_type=jnp.float32)

    def particles(kind, side, field):
        return mbuf[kind, pl.ds(side * 2, 2), :, field].reshape(pair, half)

    def gram(left, right):
        total = jnp.zeros((pair, pair), jnp.float32)
        for kind in range(2):
            for field in range(fields):
                total += inner_product(particles(kind, left, field), particles(kind, right, field))
        return total

    def squares(side):
        total = jnp.zeros((pair, half), jnp.float32)
        for kind in range(2):
            for field in range(fields):
                wide = particles(kind, side, field).astype(jnp.float32)
                total += wide * wide
        ones = jnp.ones((8, half), jnp.bfloat16)
        upper = total.astype(jnp.bfloat16)
        rest = total - upper.astype(jnp.float32)
        middle = rest.astype(jnp.bfloat16)
        lower = (rest - middle.astype(jnp.float32)).astype(jnp.bfloat16)
        return (
            inner_product(ones, upper) + inner_product(ones, middle) + inner_product(ones, lower)
        )

    def rs_copy(slot, k):
        to = (chip + k) % chips
        return remote(
            part.at[slot, to], inbox.at[slot, chip], rs_send.at[slot, k],
            rs_recv.at[slot, chip], at_chip(z, to, core),
        )

    def share(slot, total, norms):
        for q in range(chips):
            part[slot, q, :8] = norms
            part[slot, q, 8:8 + strip] = total[q * strip:(q + 1) * strip]
            part[slot, q, 8 + strip:] = total[slab + q * strip:slab + (q + 1) * strip]
        for k in range(1, chips):
            rs_copy(slot, k).start()

    def collect(slot):
        total = part[slot, chip]
        for k in range(1, chips):
            source = (chip + chips - k) % chips
            remote(
                part.at[slot, chip], inbox.at[slot, source], rs_send.at[slot, k],
                rs_recv.at[slot, source], at_chip(z, source, core),
            ).wait_recv()
            total = total + inbox[slot, source]
        return total

    def swap():
        return remote(swap_out, swap_in, s_sem.at[0], s_sem.at[1], at(mate, g))

    def k_send_copy(a, k, kind):
        to = (g * planes + y + k) % peers
        layer = near * 2 + a
        if kind == 0:
            src, dst = krow.at[a], kin.at[chip]
        elif kind == 1:
            src, dst = krow.at[a], kin_wide.at[chip]
        else:
            src, dst = krow.at[:, :, pl.ds(a * slab, slab)], kin_tall.at[:, chip]
        return remote(
            src, dst, k_send.at[a, k], k_recv.at[0 if kind == 0 else 1, chip],
            (layer * group + to // planes, to % planes),
        )

    def k_local(a, kind):
        if kind == 0:
            src, dst = krow.at[a], kin.at[chip]
        elif kind == 1:
            src, dst = krow.at[a], kin_wide.at[chip]
        else:
            src, dst = krow.at[:, :, pl.ds(a * slab, slab)], kin_tall.at[:, chip]
        return pltpu.make_async_copy(src, dst, k_recv.at[0 if kind == 0 else 1, chip])

    kinds = (
        (0, even),
        (1, both(odd, near == 0)),
        (2, both(odd, near == 1)),
    )

    def k_all(verb):
        for kind, mine in kinds:
            @pl.when(mine)
            def _():
                for a in range(2):
                    def step(k, carry):
                        getattr(k_send_copy(a, k, kind), verb)()
                        return carry

                    lax.fori_loop(1, peers, step, 0)
                    here = near * 2 + a == z

                    @pl.when(jnp.logical_not(here))
                    def _():
                        getattr(k_send_copy(a, 0, kind), verb)()

                    if verb == "start":
                        @pl.when(here)
                        def _():
                            k_local(a, kind).start()

    @pl.when(inner)
    def _():
        m_wait(z, True)
        m_wait(mate, False)
        own_go(0)
        own_go(1)
        m_wait(tip, False)
        own_go(2)
        own_go(3)
        m_wait(far_tip, False)
        f_copy(1 - core, z).wait_recv()
        f_copy(1 - core, tip).wait_recv()

        @pl.when(even)
        def _():
            share(0, gram(near, near), squares(near))

        f_copy(1 - core, mate).wait_recv()
        f_copy(1 - core, far_tip).wait_recv()

        @pl.when(even)
        def _():
            share(1, gram(far, far), squares(far))

        @pl.when(odd)
        def _():
            lower_norms, upper_norms = squares(0), squares(1)
            norms = jnp.concatenate((lower_norms[:4], upper_norms[:4]), axis=0)
            share(1, gram(0, 1), norms)

        for s in range(2):
            pass_on(s, tip, 0)
            pass_on(s, mate, 1)
        for s in range(chunks):
            decode(s, z)
        swap_out[...] = collect(1)
        swap().start()
        for s in range(2, chunks):
            pass_on(s, tip, 0)
            pass_on(s, mate, 1)
        pass_on(0, far_tip, 1)

        @pl.when(even)
        def _():
            base[...] = collect(0)

        @pl.when(odd)
        def _():
            base[...] = swap_out[...]

        for s in range(chunks):
            decode(s, tip)
        swap().wait_recv()
        total = base[...] + swap_in[...]
        gram_rows = total[8:]
        local = lax.broadcasted_iota(jnp.int32, (2 * strip, pair), 0)
        index = jnp.where(local < strip, local, local - strip + slab) + chip * strip
        lanes = lax.broadcasted_iota(jnp.int32, (2 * strip, pair), 1)
        own = jnp.sum(jnp.where(index == lanes, total[0:1], 0.0), axis=1, keepdims=True)
        distance = own + total[4:5] - 2.0 * gram_rows
        divisor = jnp.full(distance.shape, scale * total_cells, jnp.float32)
        krow[...] = jnp.exp(-distance / divisor).astype(jnp.bfloat16).reshape(2, strip, pair)
        k_all("start")
        for s in range(chunks):
            decode(s, mate)

    @pl.when(is_end)
    def _():
        for s in range(chunks):
            own_go(s)
        for s in range(chunks):
            decode(s, z)
        for layer in (toward, layers - 1 - toward):
            for s in range(chunks):
                z_copy(s, layer, 0).wait_recv()
                decode(s, layer)

    def k_wait(kind):
        for q in range(chips):
            if kind == 0:
                dst = kin.at[q]
            elif kind == 1:
                dst = kin_wide.at[q]
            else:
                dst = kin_tall.at[:, q]
            src = krow.at[:, :, pl.ds(0, slab)] if kind == 2 else krow.at[0]
            remote(
                src, dst, k_send.at[0, 0], k_recv.at[0 if kind == 0 else 1, q], at(z, back(1))
            ).wait_recv()

    k_wait(0)

    @pl.when(near == 0)
    def _():
        k_wait(1)
        kfull[:, :pair] = kin[...].reshape(slab, pair)
        kfull[:, pair:] = kin_wide[...].reshape(slab, pair)

    @pl.when(near == 1)
    def _():
        k_wait(2)
        kfull[:, pair:] = kin[...].reshape(slab, pair)
        tall = kin_tall[...].reshape(pair, slab).astype(jnp.float32)
        kfull[:, :pair] = tall.T.astype(jnp.bfloat16)

    def o_copy(s, k):
        field, side = s // 2, s % 2
        to = ring(k)
        span = pl.ds(pl.multiple_of(g * cells + side * half, 128), half)
        return remote(
            outbox.at[s, to], out_ref.at[field, :, span], o_send.at[s, k], o_recv.at[s, g],
            at(z, to),
        )

    for s in range(chunks):
        field, side = s // 2, s % 2

        @pl.when(inner)
        def _():
            if s > 0:
                pass_on(s, far_tip, 1)
            decode(s, far_tip)

        @pl.when(is_end)
        def _():
            z_copy(s, mate, 0).wait_recv()
            decode(s, mate)

        kernel = kfull[...]
        update = jnp.dot(
            kernel, high[s].reshape(count, half), preferred_element_type=jnp.float32
        ) + jnp.dot(kernel, low[s].reshape(count, half), preferred_element_type=jnp.float32)
        outbox[s] = update.reshape(group, rows, half)
        for k in range(1, group):
            o_copy(s, k).start()
        span = pl.ds(pl.multiple_of(g * cells + side * half, 128), half)
        out_ref[field, :, span] = outbox[s, g]

    mine = kfull[pl.ds(pl.multiple_of(g * rows, rows), rows)].astype(jnp.float32)
    rowsum = jnp.sum(mine, axis=1, keepdims=True)
    factor_ref[...] = 2.0 / jnp.full(factor_ref.shape, scale, jnp.float32) * rowsum

    for slot, side in ((0, far), (1, near)):
        for k in range(group):
            if slot == 1 and k == 0:
                @pl.when(is_end)
                def _():
                    m_copy(1, near, 0).wait_send()
            else:
                m_copy(slot, side, k).wait_send()
    for s in range(chunks):
        for k in range(1, group):
            a_copy(s, k).wait_send()
        z_copy(s, z, 0).wait_send()

    @pl.when(inner)
    def _():
        for layer in range(layers):
            f_copy(core, layer).wait_send()
        for s in range(chunks):
            z_copy(s, z, 1).wait_send()
            z_copy(s, tip, 0).wait_send()
            z_copy(s, mate, 1).wait_send()
            z_copy(s, far_tip, 1).wait_send()
        for k in range(1, chips):
            rs_copy(1, k).wait_send()

        @pl.when(even)
        def _():
            for k in range(1, chips):
                rs_copy(0, k).wait_send()

        swap().wait_send()
        k_all("wait_send")

    for s in range(chunks):
        field, side = s // 2, s % 2
        for k in range(1, group):
            o_copy(s, k).wait_send()
            source = back(k)
            span = pl.ds(pl.multiple_of(source * cells + side * half, 128), half)
            remote(
                outbox.at[s, source], out_ref.at[field, :, span], o_send.at[s, k],
                o_recv.at[s, source], at(z, source),
            ).wait_recv()


def fused_body(layers, group, planes, models, gradients, length_scale):
    fields, rows, width = models.shape
    cells = width // group
    half = cells // 2
    slab = group * rows
    count = layers * slab
    chips = group // 2 * planes
    strip = slab // chips
    chunks = fields * 2
    pair = 2 * slab
    peers = group * planes
    dma = pltpu.SemaphoreType.DMA
    vmem = pltpu.VMEM
    gathered, factor = pl.pallas_call(
        functools.partial(stein_kernel, layers, group, planes),
        out_shape=(
            jax.ShapeDtypeStruct(models.shape, jnp.float32),
            jax.ShapeDtypeStruct((rows, 128), jnp.float32),
        ),
        in_specs=[
            pl.BlockSpec(memory_space=pltpu.SMEM),
            pl.BlockSpec(memory_space=pl.ANY),
            pl.BlockSpec(memory_space=pl.ANY),
        ],
        out_specs=(
            pl.BlockSpec(memory_space=pltpu.VMEM),
            pl.BlockSpec(memory_space=pltpu.VMEM),
        ),
        scratch_shapes=[
            vmem(models.shape, jnp.bfloat16),
            vmem(models.shape, jnp.bfloat16),
            vmem((chunks, group, rows, half), jnp.bfloat16),
            vmem((2, layers, group, fields, rows, half), jnp.bfloat16),
            vmem((chunks, layers, group, rows, half), jnp.bfloat16),
            vmem((chunks, layers, slab, half), jnp.bfloat16),
            vmem((chunks, layers, slab, half), jnp.bfloat16),
            vmem((2, chips, 8 + 2 * strip, pair), jnp.float32),
            vmem((2, chips, 8 + 2 * strip, pair), jnp.float32),
            vmem((8 + 2 * strip, pair), jnp.float32),
            vmem((8 + 2 * strip, pair), jnp.float32),
            vmem((8 + 2 * strip, pair), jnp.float32),
            vmem((2, strip, pair), jnp.bfloat16),
            vmem((chips, strip, pair), jnp.bfloat16),
            vmem((chips, strip, pair), jnp.bfloat16),
            vmem((2, chips, strip, slab), jnp.bfloat16),
            vmem((slab, count), jnp.bfloat16),
            vmem((chunks, group, rows, half), jnp.float32),
            dma((3,)),
            dma((2, group)),
            dma((layers, group)),
            dma((layers,)),
            dma((layers,)),
            dma((chunks, group)),
            dma((chunks, group)),
            dma((2, chunks, layers)),
            dma((chunks, layers)),
            dma((2, chips)),
            dma((2, chips)),
            dma((2,)),
            dma((2, peers)),
            dma((2, chips)),
            dma((chunks, group)),
            dma((chunks, group)),
        ],
        compiler_params=pltpu.CompilerParams(collective_id=0, has_side_effects=True),
        name="stein",
    )(length_scale, models, gradients)
    own = factor[None, :, :1] * models.astype(jnp.float32)
    return (gathered * (1.0 / LIFT) + own) * (1.0 / count)


def solution(mesh):
    spread, planes = mesh.shape["dom"], mesh.shape["cell"]
    layers = math.isqrt(spread)
    group = spread // layers

    def body(models, gradients, length_scale):
        _, rows, width = models.shape
        slab = group * rows
        chips = group // 2 * planes
        fits = (
            layers == 4
            and group % 2 == 0
            and models.shape[0] == 2
            and layers * group == spread
            and width % (group * 256) == 0
            and rows % 16 == 0
            and slab % 128 == 0
            and slab % (chips * 16) == 0
        )
        if not fits:
            return plain_body(models, gradients, length_scale)
        return fused_body(layers, group, planes, models, gradients, length_scale)

    placed = (P(None, "dom", "cell"), P(None, "dom", "cell"), P())
    return jax.shard_map(
        body, mesh=mesh, in_specs=placed, out_specs=P(None, "dom", "cell"), check_vma=False
    )
```

```python
import functools
import math

import jax
import jax.numpy as jnp
from jax import lax
from jax.experimental import pallas as pl
from jax.experimental.pallas import tpu as pltpu
from jax.sharding import PartitionSpec as P

MESH = pl.DeviceIdType.MESH


def plain_body(models, gradients, length_scale):
    local_models, local_grads = (
        lax.all_to_all(models, "dom", split_axis=2, concat_axis=1, tiled=True),
        lax.all_to_all(gradients, "dom", split_axis=2, concat_axis=1, tiled=True),
    )
    cell_block = local_models.shape[2]
    particles = local_models.shape[1]
    cell_count = cell_block * lax.axis_size("dom") * lax.axis_size("cell")
    scale_value = length_scale[0]
    divisor = scale_value * cell_count
    partial_value = jnp.einsum(
        "kpc,kqc->pq", local_models, local_models, preferred_element_type=jnp.float32
    )
    summed = lax.psum(partial_value, "cell")
    row_block = lax.psum_scatter(summed, "dom", scatter_dimension=0, tiled=True)
    row_count = row_block.shape[0]
    row_start = lax.axis_index("dom") * row_count
    own_squares = jnp.diagonal(lax.dynamic_slice_in_dim(row_block, row_start, row_count, 1))
    squares = lax.all_gather(own_squares, "dom", axis=0, tiled=True)
    distance = own_squares[:, None] + squares[None, :] - 2.0 * row_block
    kernel = lax.all_gather(
        jnp.exp(-distance / divisor).astype(jnp.bfloat16), "dom", axis=0, tiled=True
    )
    rowsum = jnp.sum(kernel.astype(jnp.float32), axis=1)
    stacked = jnp.concatenate((local_grads, local_models), axis=2)
    product = jnp.einsum("pq,kqc->kpc", kernel, stacked, preferred_element_type=jnp.float32)
    attract = product[:, :, :cell_block]
    pulled = product[:, :, cell_block:]
    update = (
        attract
        + 2.0 / scale_value * (rowsum[None, :, None] * local_models.astype(jnp.float32) - pulled)
    ) / particles
    return lax.all_to_all(update, "dom", split_axis=1, concat_axis=2, tiled=True)


LIFT = 512.0


def stein_kernel(
    layers, group, planes,
    scale_ref, models_ref, grads_ref, out_ref,
    m_loc, g_loc, code, mst, mbuf, hbuf, high, low, part, inbox, swap_out, swap_in,
    krow, kin, kfull, outbox,
    ready, loc_sem, m_send, m_recv, mz_send, mz_recv, f_send, f_recv, a_send, a_recv, z_send, z_recv,
    rs_send, rs_recv, s_send, s_recv, k_send, k_recv, o_send, o_recv,
):
    fields, rows, width = models_ref.shape
    cells = width // group
    half = cells // 2
    slab = group * rows
    count = layers * slab
    chips = group // 2 * planes
    peers = group * planes
    strip = slab // chips
    chunks = fields * 2
    pair = 2 * slab
    total_cells = width * planes
    dom = lax.axis_index("dom")
    y = lax.axis_index("cell")
    z = dom // group
    g = dom % group
    core = g % 2
    chip = g // 2 * planes + y
    near = z // 2
    far = 1 - near
    inner = jnp.logical_and(z > 0, z < layers - 1)
    is_end = jnp.logical_not(inner)
    mate = layers - 1 - z
    tip = near * (layers - 1)
    far_tip = far * (layers - 1)
    toward = jnp.where(inner, mate, 1 + near)
    even = core == 0
    odd = core == 1

    def both(left, right):
        return jnp.logical_and(left, right)

    def at(layer, which):
        return (layer * group + which, y)

    def at_chip(layer, which, kind):
        return (layer * group + which // planes * 2 + kind, which % planes)

    def ring(k):
        return (g + k) % group

    def back(k):
        return (g + group - k) % group

    def remote(src, dst, send, recv, device):
        return pltpu.make_async_remote_copy(
            src_ref=src, dst_ref=dst, send_sem=send, recv_sem=recv,
            device_id=device, device_id_type=MESH,
        )

    loads = [
        pltpu.make_async_copy(models_ref, m_loc, loc_sem.at[0]),
        pltpu.make_async_copy(grads_ref, g_loc, loc_sem.at[1]),
    ]
    for copy in loads:
        copy.start()

    barrier = pltpu.get_barrier_semaphore()
    here = g * planes + y

    def greet(k, carry):
        to = (here + k) % peers
        pl.semaphore_signal(
            barrier, inc=1, device_id=(z * group + to // planes, to % planes), device_id_type=MESH
        )
        return carry

    lax.fori_loop(1, peers, greet, 0)
    pl.semaphore_signal(barrier, inc=1, device_id=at(toward, g), device_id_type=MESH)

    @pl.when(inner)
    def _():
        pl.semaphore_signal(barrier, inc=1, device_id=at(tip, g), device_id_type=MESH)

    pl.semaphore_wait(barrier, peers + jnp.where(inner, 1, 0))

    @pl.when(inner)
    def _():
        pl.semaphore_signal(ready, inc=1, device_id=at(tip, g), device_id_type=MESH)

    def m_part(side, to):
        return models_ref.at[:, :, pl.ds(pl.multiple_of(to * cells + side * half, 128), half)]

    sides = (far, near)

    def landing(slot, kind, source):
        return mbuf.at[kind, z, source] if slot else mst.at[source]

    def m_copy(slot, k):
        to = ring(k)
        return remote(
            m_part(sides[slot], to), landing(slot, to % 2, g),
            m_send.at[slot, k], m_recv.at[slot, g], at(z, to),
        )

    def m_own(slot):
        return pltpu.make_async_copy(
            m_part(sides[slot], g), landing(slot, core, g), loc_sem.at[2 + slot]
        )

    def m_hop(slot, k):
        source = back(k)
        src = m_part(sides[slot], g) if k == 0 else landing(slot, core, source)
        return remote(
            src, mbuf.at[core, z, source], mz_send.at[slot, k], mz_recv.at[z, source],
            at(1 + sides[slot], g),
        )

    def m_ready(slot, k):
        source = back(k)
        remote(
            m_part(sides[slot], g), landing(slot, core, source),
            m_send.at[slot, k], m_recv.at[slot, source], at(z, source),
        ).wait_recv()

    for slot in range(2):
        for k in range(1, group):
            m_copy(slot, k).start()
        m_own(slot).start()

    @pl.when(is_end)
    def _():
        m_hop(1, 0).start()
        pl.semaphore_wait(ready, 1)

    m_hop(0, 0).start()

    for copy in loads:
        copy.wait()

    scale = scale_ref[0]

    def a_copy(s, k):
        to = ring(k)
        return remote(
            code.at[s, to], hbuf.at[s, z, g], a_send.at[s, k], a_recv.at[s, g], at(z, to)
        )

    weight = 2.0 * LIFT / jnp.full((rows, half), scale, jnp.float32)
    for s in range(chunks):
        field, side = s // 2, s % 2
        for to in range(group):
            span = slice(to * cells + side * half, to * cells + side * half + half)
            value = g_loc[field, :, span].astype(jnp.float32) * LIFT
            value = value - weight * m_loc[field, :, span].astype(jnp.float32)
            square = value * value
            code[s, to] = (square * square * square * value * jnp.abs(value)).astype(jnp.bfloat16)
        for k in range(1, group):
            a_copy(s, k).start()
        hbuf[s, z, g] = code[s, g]

    def z_copy(s, layer, outward):
        block = hbuf.at[s, layer]
        return remote(
            block, block, z_send.at[outward, s, layer], z_recv.at[s, layer],
            at(tip if outward else toward, g),
        )

    def decode(s, layer):
        value = hbuf[s, layer].reshape(slab, half).astype(jnp.float32)
        root = jnp.exp2(jnp.log2(jnp.abs(value)) * 0.125)
        root = jnp.where(value < 0.0, -root, root)
        upper = root.astype(jnp.bfloat16)
        high[s, layer] = upper
        low[s, layer] = (root - upper.astype(jnp.float32)).astype(jnp.bfloat16)

    def own_ready(s):
        for k in range(1, group):
            source = back(k)
            remote(
                code.at[s, g], hbuf.at[s, z, source], a_send.at[s, k], a_recv.at[s, source],
                at(z, source),
            ).wait_recv()

    def pass_on(s, layer, outward):
        z_copy(s, layer, outward).wait_recv()
        z_copy(s, layer, outward).start()

    def f_copy(kind, layer):
        block = mbuf.at[kind, layer]
        return remote(
            block, block, f_send.at[layer], f_recv.at[layer], at(z, g + 1 - 2 * core)
        )

    def m_wait(layer):
        for k in range(group):
            source = back(k)
            remote(
                m_part(near, g), mbuf.at[core, layer, source], mz_send.at[0, k],
                mz_recv.at[layer, source], at(layer, g),
            ).wait_recv()
        f_copy(core, layer).start()

    contract = (((1,), (1,)), ((), ()))

    def inner_product(left, right):
        return lax.dot_general(left, right, contract, preferred_element_type=jnp.float32)

    def particles(kind, side, field):
        return mbuf[kind, pl.ds(side * 2, 2), :, field].reshape(pair, half)

    def gram(left, right):
        total = jnp.zeros((pair, pair), jnp.float32)
        for kind in range(2):
            for field in range(fields):
                total += inner_product(particles(kind, left, field), particles(kind, right, field))
        return total

    def squares(side):
        total = jnp.zeros((pair, half), jnp.float32)
        for kind in range(2):
            for field in range(fields):
                wide = particles(kind, side, field).astype(jnp.float32)
                total += wide * wide
        ones = jnp.ones((8, half), jnp.bfloat16)
        upper = total.astype(jnp.bfloat16)
        rest = total - upper.astype(jnp.float32)
        middle = rest.astype(jnp.bfloat16)
        lower = (rest - middle.astype(jnp.float32)).astype(jnp.bfloat16)
        return (
            inner_product(ones, upper) + inner_product(ones, middle) + inner_product(ones, lower)
        )

    def rs_copy(slot, k):
        to = (chip + k) % chips
        return remote(
            part.at[slot, to], inbox.at[slot, chip], rs_send.at[slot, k],
            rs_recv.at[slot, chip], at_chip(z, to, core),
        )

    def share(slot, total, norms):
        for q in range(chips):
            part[slot, q, :8] = norms
            part[slot, q, 8:8 + strip] = total[q * strip:(q + 1) * strip]
            part[slot, q, 8 + strip:] = total[slab + q * strip:slab + (q + 1) * strip]
        for k in range(1, chips):
            rs_copy(slot, k).start()

    def collect(slot):
        total = part[slot, chip]
        for k in range(1, chips):
            source = (chip + chips - k) % chips
            remote(
                part.at[slot, chip], inbox.at[slot, source], rs_send.at[slot, k],
                rs_recv.at[slot, source], at_chip(z, source, core),
            ).wait_recv()
            total = total + inbox[slot, source]
        return total

    def swap(layer, source):
        return remote(
            swap_out.at[layer], swap_in.at[source], s_send.at[layer], s_recv.at[source],
            at(layer, g),
        )

    def swap_rows(layer, total, row):
        swap_out[layer, :8] = total[:8]
        swap_out[layer, 8:] = total[8 + row * strip:8 + (row + 1) * strip]

    def swap_columns(layer, total, column):
        span = slice(column * slab, (column + 1) * slab)
        swap_out[layer, :8] = total[:8]
        swap_out[layer, 8:] = jnp.concatenate(
            (total[8:8 + strip, span], total[8 + strip:, span]), axis=1
        )

    def k_copy(k):
        to = (here + k) % peers
        return remote(
            krow, kin.at[core, chip], k_send.at[k], k_recv.at[core, chip],
            (z * group + to // planes, to % planes),
        )

    def k_spread(verb):
        def step(k, carry):
            getattr(k_copy(k), verb)()
            return carry

        lax.fori_loop(1, peers, step, 0)

    def k_rows(total):
        lanes = lax.broadcasted_iota(jnp.int32, (strip, pair), 1)
        local = lax.broadcasted_iota(jnp.int32, (strip, pair), 0) + chip * strip
        norms = total[0:1]
        first = jnp.sum(jnp.where(lanes == local, norms, 0.0), axis=1, keepdims=True)
        second = jnp.sum(jnp.where(lanes == local + slab, norms, 0.0), axis=1, keepdims=True)
        tall = both(odd, near == 1)
        left = lanes < slab
        upper = z % 2 == 1
        pick = jnp.where(tall, left.astype(jnp.int32), jnp.where(upper, 0, 1))
        own = jnp.where(pick == 1, first, second)
        others = total[4:5]
        low_half = jnp.concatenate((others[:, :slab], others[:, :slab]), axis=1)
        high_half = jnp.concatenate((others[:, slab:], others[:, slab:]), axis=1)
        others = jnp.where(tall, jnp.where(upper, high_half, low_half), others)
        distance = own + others - 2.0 * total[8:]
        divisor = jnp.full(distance.shape, scale * total_cells, jnp.float32)
        krow[...] = jnp.exp(-distance / divisor).astype(jnp.bfloat16)
        k_spread("start")
        kin[core, chip] = krow[...]

    for k in range(1, group):
        m_ready(0, k)
        m_hop(0, k).start()

    @pl.when(is_end)
    def _():
        for k in range(1, group):
            m_ready(1, k)
            m_hop(1, k).start()

    @pl.when(inner)
    def _():
        for k in range(1, group):
            m_ready(1, k)
        m_own(1).wait()
        f_copy(core, z).start()
        for s in range(chunks):
            own_ready(s)
            z_copy(s, z, 1).start()
        z_copy(0, z, 0).start()
        z_copy(1, z, 0).start()
        z_copy(2, z, 0).start()
        z_copy(3, z, 0).start()
        m_wait(mate)
        m_wait(tip)
        m_wait(far_tip)
        f_copy(1 - core, z).wait_recv()
        f_copy(1 - core, tip).wait_recv()

        @pl.when(even)
        def _():
            share(0, gram(near, near), squares(near))

        f_copy(1 - core, mate).wait_recv()
        f_copy(1 - core, far_tip).wait_recv()

        @pl.when(even)
        def _():
            share(1, gram(far, far), squares(far))

        @pl.when(odd)
        def _():
            lower_norms, upper_norms = squares(0), squares(1)
            norms = jnp.concatenate((lower_norms[:4], upper_norms[:4]), axis=0)
            share(1, gram(0, 1), norms)

        for s in range(2):
            pass_on(s, tip, 0)
        for s in range(4):
            pass_on(s, mate, 1)
        for s in range(chunks):
            decode(s, z)

        @pl.when(even)
        def _():
            near_total = collect(0)
            swap_rows(near * 2, near_total, 0)
            swap_rows(near * 2 + 1, near_total, 1)
            swap(tip, near).start()
            far_total = collect(1)
            swap_rows(far * 2, far_total, 0)
            swap_rows(far * 2 + 1, far_total, 1)

        @pl.when(odd)
        def _():
            total = collect(1)
            swap_rows(0, total, 0)
            swap_rows(1, total, 1)
            swap_columns(2, total, 0)
            swap_columns(3, total, 1)
            swap(tip, near).start()

        swap(far_tip, near).start()
        swap(mate, near).start()
        for s in range(2, chunks):
            pass_on(s, tip, 0)
        for s in range(4, chunks):
            pass_on(s, mate, 1)
        for s in range(1):
            pass_on(s, far_tip, 1)
        for s in range(chunks):
            decode(s, tip)
        swap(mate, far).wait_recv()
        k_rows(swap_out[z] + swap_in[far])
        for s in range(1, chunks):
            pass_on(s, far_tip, 1)
        for s in range(chunks):
            decode(s, mate)

    @pl.when(is_end)
    def _():
        m_own(1).wait()
        for s in range(chunks):
            own_ready(s)
            z_copy(s, z, 0).start()
        for s in range(chunks):
            decode(s, z)
        for layer in (toward, layers - 1 - toward):
            for s in range(chunks):
                z_copy(s, layer, 0).wait_recv()
                decode(s, layer)
        swap(toward, near).wait_recv()
        swap(mate, far).wait_recv()
        k_rows(swap_in[0] + swap_in[1])

    def k_ready(kind, k):
        q = (chip + k) % chips
        remote(
            krow, kin.at[kind, q], k_send.at[0], k_recv.at[kind, q], at(z, back(1))
        ).wait_recv()

    k_ready(1 - core, 0)
    for k in range(1, chips):
        k_ready(0, k)
        k_ready(1, k)

    @pl.when(near == 0)
    def _():
        kfull[:, :pair] = kin[0].reshape(slab, pair)
        kfull[:, pair:] = kin[1].reshape(slab, pair)

    @pl.when(near == 1)
    def _():
        kfull[:, pair:] = kin[0].reshape(slab, pair)
        tall = kin[1].reshape(slab, pair).astype(jnp.float32)
        kfull[:, :slab] = tall[:, :slab].T.astype(jnp.bfloat16)
        kfull[:, slab:pair] = tall[:, slab:].T.astype(jnp.bfloat16)

    rowsum = jnp.sum(kfull[...].astype(jnp.float32), axis=1, keepdims=True)
    pull = 2.0 / jnp.full((slab, 1), scale, jnp.float32) * rowsum
    m_own(0).wait()

    def o_copy(s, k):
        field, side = s // 2, s % 2
        to = ring(k)
        span = pl.ds(pl.multiple_of(g * cells + side * half, 128), half)
        return remote(
            outbox.at[s, to], out_ref.at[field, :, span], o_send.at[s, k], o_recv.at[s, g],
            at(z, to),
        )

    for s in range(chunks):
        field, side = s // 2, s % 2

        @pl.when(inner)
        def _():
            decode(s, far_tip)

        @pl.when(is_end)
        def _():
            z_copy(s, mate, 0).wait_recv()
            decode(s, mate)

        kernel = kfull[...]
        update = jnp.dot(
            kernel, high[s].reshape(count, half), preferred_element_type=jnp.float32
        ) + jnp.dot(kernel, low[s].reshape(count, half), preferred_element_type=jnp.float32)
        own = jnp.where(near == side, mbuf[core, z, :, field], mst[:, field])
        own = own.reshape(slab, half).astype(jnp.float32)
        update = update * (1.0 / LIFT) + pull * own
        square = update * update
        update = square * square * square * update * jnp.abs(update)
        outbox[s] = update.astype(jnp.bfloat16).reshape(group, rows, half)
        for k in range(1, group):
            o_copy(s, k).start()
        span = pl.ds(pl.multiple_of(g * cells + side * half, 128), half)
        out_ref[field, :, span] = outbox[s, g]

    for k in range(1, group):
        m_copy(0, k).wait_send()
        m_copy(1, k).wait_send()
    for k in range(group):
        m_hop(0, k).wait_send()

    @pl.when(is_end)
    def _():
        for k in range(group):
            m_hop(1, k).wait_send()
    for s in range(chunks):
        for k in range(1, group):
            a_copy(s, k).wait_send()
        z_copy(s, z, 0).wait_send()

    @pl.when(inner)
    def _():
        for layer in range(layers):
            f_copy(core, layer).wait_send()
        for s in range(chunks):
            z_copy(s, z, 1).wait_send()
            z_copy(s, tip, 0).wait_send()
            z_copy(s, mate, 1).wait_send()
            z_copy(s, far_tip, 1).wait_send()
        for k in range(1, chips):
            rs_copy(1, k).wait_send()

        @pl.when(even)
        def _():
            for k in range(1, chips):
                rs_copy(0, k).wait_send()

        swap(tip, near).wait_send()
        swap(far_tip, near).wait_send()
        swap(mate, near).wait_send()

    k_spread("wait_send")

    for s in range(chunks):
        field, side = s // 2, s % 2
        for k in range(1, group):
            o_copy(s, k).wait_send()
            source = back(k)
            span = pl.ds(pl.multiple_of(source * cells + side * half, 128), half)
            remote(
                outbox.at[s, source], out_ref.at[field, :, span], o_send.at[s, k],
                o_recv.at[s, source], at(z, source),
            ).wait_recv()


def fused_body(layers, group, planes, models, gradients, length_scale):
    fields, rows, width = models.shape
    cells = width // group
    half = cells // 2
    slab = group * rows
    count = layers * slab
    chips = group // 2 * planes
    strip = slab // chips
    chunks = fields * 2
    pair = 2 * slab
    peers = group * planes
    dma = pltpu.SemaphoreType.DMA
    vmem = pltpu.VMEM
    gathered = pl.pallas_call(
        functools.partial(stein_kernel, layers, group, planes),
        out_shape=jax.ShapeDtypeStruct(models.shape, jnp.bfloat16),
        in_specs=[
            pl.BlockSpec(memory_space=pltpu.SMEM),
            pl.BlockSpec(memory_space=pl.ANY),
            pl.BlockSpec(memory_space=pl.ANY),
        ],
        out_specs=pl.BlockSpec(memory_space=pltpu.VMEM),
        scratch_shapes=[
            vmem(models.shape, jnp.bfloat16),
            vmem(models.shape, jnp.bfloat16),
            vmem((chunks, group, rows, half), jnp.bfloat16),
            vmem((group, fields, rows, half), jnp.bfloat16),
            vmem((2, layers, group, fields, rows, half), jnp.bfloat16),
            vmem((chunks, layers, group, rows, half), jnp.bfloat16),
            vmem((chunks, layers, slab, half), jnp.bfloat16),
            vmem((chunks, layers, slab, half), jnp.bfloat16),
            vmem((2, chips, 8 + 2 * strip, pair), jnp.float32),
            vmem((2, chips, 8 + 2 * strip, pair), jnp.float32),
            vmem((layers, 8 + strip, pair), jnp.float32),
            vmem((2, 8 + strip, pair), jnp.float32),
            vmem((strip, pair), jnp.bfloat16),
            vmem((2, chips, strip, pair), jnp.bfloat16),
            vmem((slab, count), jnp.bfloat16),
            vmem((chunks, group, rows, half), jnp.bfloat16),
            pltpu.SemaphoreType.REGULAR,
            dma((4,)),
            dma((2, group)),
            dma((2, group)),
            dma((2, group)),
            dma((layers, group)),
            dma((layers,)),
            dma((layers,)),
            dma((chunks, group)),
            dma((chunks, group)),
            dma((2, chunks, layers)),
            dma((chunks, layers)),
            dma((2, chips)),
            dma((2, chips)),
            dma((layers,)),
            dma((2,)),
            dma((peers,)),
            dma((2, chips)),
            dma((chunks, group)),
            dma((chunks, group)),
        ],
        compiler_params=pltpu.CompilerParams(collective_id=0, has_side_effects=True),
        name="stein",
    )(length_scale, models, gradients)
    wide = gathered.astype(jnp.float32)
    root = jnp.exp2(jnp.log2(jnp.abs(wide)) * 0.125) * (1.0 / count)
    return jnp.where(wide < 0.0, -root, root)


def solution(mesh):
    spread, planes = mesh.shape["dom"], mesh.shape["cell"]
    layers = math.isqrt(spread)
    group = spread // layers

    def body(models, gradients, length_scale):
        _, rows, width = models.shape
        slab = group * rows
        chips = group // 2 * planes
        fits = (
            layers == 4
            and group % 2 == 0
            and models.shape[0] == 2
            and layers * group == spread
            and width % (group * 256) == 0
            and rows % 16 == 0
            and slab % 128 == 0
            and slab % (chips * 16) == 0
        )
        if not fits:
            return plain_body(models, gradients, length_scale)
        return fused_body(layers, group, planes, models, gradients, length_scale)

    placed = (P(None, "dom", "cell"), P(None, "dom", "cell"), P())
    return jax.shard_map(
        body, mesh=mesh, in_specs=placed, out_specs=P(None, "dom", "cell"), check_vma=False
    )
```

```python
import functools
import math

import jax
import jax.numpy as jnp
from jax import lax
from jax.experimental import pallas as pl
from jax.experimental.pallas import tpu as pltpu
from jax.sharding import PartitionSpec as P

MESH = pl.DeviceIdType.MESH


def plain_body(models, gradients, length_scale):
    local_models, local_grads = (
        lax.all_to_all(models, "dom", split_axis=2, concat_axis=1, tiled=True),
        lax.all_to_all(gradients, "dom", split_axis=2, concat_axis=1, tiled=True),
    )
    cell_block = local_models.shape[2]
    particles = local_models.shape[1]
    cell_count = cell_block * lax.axis_size("dom") * lax.axis_size("cell")
    scale_value = length_scale[0]
    divisor = scale_value * cell_count
    partial_value = jnp.einsum(
        "kpc,kqc->pq", local_models, local_models, preferred_element_type=jnp.float32
    )
    summed = lax.psum(partial_value, "cell")
    row_block = lax.psum_scatter(summed, "dom", scatter_dimension=0, tiled=True)
    row_count = row_block.shape[0]
    row_start = lax.axis_index("dom") * row_count
    own_squares = jnp.diagonal(lax.dynamic_slice_in_dim(row_block, row_start, row_count, 1))
    squares = lax.all_gather(own_squares, "dom", axis=0, tiled=True)
    distance = own_squares[:, None] + squares[None, :] - 2.0 * row_block
    kernel = lax.all_gather(
        jnp.exp(-distance / divisor).astype(jnp.bfloat16), "dom", axis=0, tiled=True
    )
    rowsum = jnp.sum(kernel.astype(jnp.float32), axis=1)
    stacked = jnp.concatenate((local_grads, local_models), axis=2)
    product = jnp.einsum("pq,kqc->kpc", kernel, stacked, preferred_element_type=jnp.float32)
    attract = product[:, :, :cell_block]
    pulled = product[:, :, cell_block:]
    update = (
        attract
        + 2.0 / scale_value * (rowsum[None, :, None] * local_models.astype(jnp.float32) - pulled)
    ) / particles
    return lax.all_to_all(update, "dom", split_axis=1, concat_axis=2, tiled=True)


LIFT = 512.0


def stein_kernel(
    layers, group, planes,
    scale_ref, models_ref, grads_ref, out_ref,
    m_loc, g_loc, code, mst, mbuf, hbuf, high, low, part, inbox, swap_out, swap_in,
    krow, kin, kfull, outbox,
    own_sem, h_send, loc_sem, m_send, m_recv, mz_send, mz_recv, f_send, f_recv, a_send, a_recv, z_send, z_recv,
    rs_send, rs_recv, s_send, s_recv, k_send, k_recv, o_send, o_recv,
):
    fields, rows, width = models_ref.shape
    cells = width // group
    half = cells // 2
    slab = group * rows
    count = layers * slab
    chips = group // 2 * planes
    peers = group * planes
    strip = slab // chips
    chunks = fields * 2
    pair = 2 * slab
    total_cells = width * planes
    dom = lax.axis_index("dom")
    y = lax.axis_index("cell")
    z = dom // group
    g = dom % group
    core = g % 2
    chip = g // 2 * planes + y
    near = z // 2
    far = 1 - near
    inner = jnp.logical_and(z > 0, z < layers - 1)
    is_end = jnp.logical_not(inner)
    mate = layers - 1 - z
    tip = near * (layers - 1)
    far_tip = far * (layers - 1)
    toward = jnp.where(inner, mate, 1 + near)
    even = core == 0
    odd = core == 1

    def both(left, right):
        return jnp.logical_and(left, right)

    def at(layer, which):
        return (layer * group + which, y)

    def at_chip(layer, which, kind):
        return (layer * group + which // planes * 2 + kind, which % planes)

    def ring(k):
        return (g, g + 1 - 2 * core, (g + 2) % group, group - 1 - g)[k]

    back = ring

    def remote(src, dst, send, recv, device):
        return pltpu.make_async_remote_copy(
            src_ref=src, dst_ref=dst, send_sem=send, recv_sem=recv,
            device_id=device, device_id_type=MESH,
        )

    loads = [
        pltpu.make_async_copy(models_ref, m_loc, loc_sem.at[0]),
        pltpu.make_async_copy(grads_ref, g_loc, loc_sem.at[1]),
    ]
    for copy in loads:
        copy.start()

    barrier = pltpu.get_barrier_semaphore()
    here = g * planes + y

    def greet(k, carry):
        to = (here + k) % peers
        pl.semaphore_signal(
            barrier, inc=1, device_id=(z * group + to // planes, to % planes), device_id_type=MESH
        )
        return carry

    lax.fori_loop(1, peers, greet, 0)
    pl.semaphore_signal(barrier, inc=1, device_id=at(toward, g), device_id_type=MESH)

    @pl.when(inner)
    def _():
        pl.semaphore_signal(barrier, inc=1, device_id=at(tip, g), device_id_type=MESH)
        pl.semaphore_signal(barrier, inc=1, device_id=at(far_tip, g), device_id_type=MESH)

    pl.semaphore_wait(barrier, peers + 1)

    def m_part(side, to):
        return models_ref.at[:, :, pl.ds(pl.multiple_of(to * cells + side * half, 128), half)]

    sides = (far, near)

    def landing(slot, kind, source):
        return mbuf.at[kind, z, source] if slot else mst.at[source]

    def m_copy(slot, k):
        to = ring(k)
        return remote(
            m_part(sides[slot], to), landing(slot, to % 2, g),
            m_send.at[slot, k], m_recv.at[slot, g], at(z, to),
        )

    def m_own(slot):
        return pltpu.make_async_copy(
            m_part(sides[slot], g), landing(slot, core, g), loc_sem.at[2 + slot]
        )

    def m_hop(slot, k):
        source = back(k)
        src = m_part(sides[slot], g) if k == 0 else landing(slot, core, source)
        return remote(
            src, mbuf.at[core, z, source], mz_send.at[slot, k], mz_recv.at[z, source],
            at(1 + sides[slot], g),
        )

    def m_ready(slot, k):
        source = back(k)
        remote(
            m_part(sides[slot], g), landing(slot, core, source),
            m_send.at[slot, k], m_recv.at[slot, source], at(z, source),
        ).wait_recv()

    for slot in range(2):
        for k in range(1, group):
            m_copy(slot, k).start()
        m_own(slot).start()

    @pl.when(is_end)
    def _():
        m_hop(1, 0).start()

    m_hop(0, 0).start()

    for copy in loads:
        copy.wait()

    scale = scale_ref[0]

    def a_copy(s, k):
        to = ring(k)
        return remote(
            code.at[s, to], hbuf.at[s, z, g], a_send.at[s, k], a_recv.at[s, g], at(z, to)
        )

    weight = 2.0 * LIFT / jnp.full((rows, half), scale, jnp.float32)
    for s in range(chunks):
        field, side = s // 2, s % 2
        for to in range(group):
            span = slice(to * cells + side * half, to * cells + side * half + half)
            value = g_loc[field, :, span].astype(jnp.float32) * LIFT
            value = value - weight * m_loc[field, :, span].astype(jnp.float32)
            square = value * value
            code[s, to] = (square * square * square * value * jnp.abs(value)).astype(jnp.bfloat16)
        for k in range(1, group):
            a_copy(s, k).start()
        hbuf[s, z, g] = code[s, g]

    def z_copy(s, layer, outward):
        block = hbuf.at[s, layer]
        return remote(
            block, block, z_send.at[outward, s, layer], z_recv.at[s, layer],
            at(tip if outward else toward, g),
        )

    def decode(s, layer):
        value = hbuf[s, layer].reshape(slab, half).astype(jnp.float32)
        root = jnp.exp2(jnp.log2(jnp.abs(value)) * 0.125)
        root = jnp.where(value < 0.0, -root, root)
        upper = root.astype(jnp.bfloat16)
        high[s, layer] = upper
        low[s, layer] = (root - upper.astype(jnp.float32)).astype(jnp.bfloat16)

    def own_ready(s, first=1, last=group):
        for k in range(first, last):
            source = back(k)
            remote(
                code.at[s, g], hbuf.at[s, z, source], a_send.at[s, k], a_recv.at[s, source],
                at(z, source),
            ).wait_recv()

    def z_half(s, side):
        start = (g // 2 + side) % 2 * 2
        block = hbuf.at[s, z, pl.ds(start, 2)]
        return remote(block, block, h_send.at[side, s], z_recv.at[s, z], at(tip, g))

    def pass_on(s, layer, outward):
        z_copy(s, layer, outward).wait_recv()
        z_copy(s, layer, outward).start()

    def f_copy(kind, layer):
        block = mbuf.at[kind, layer]
        return remote(
            block, block, f_send.at[layer], f_recv.at[layer], at(z, g + 1 - 2 * core)
        )

    def m_wait(layer):
        for k in range(group):
            source = back(k)
            remote(
                m_part(near, g), mbuf.at[core, layer, source], mz_send.at[0, k],
                mz_recv.at[layer, source], at(layer, g),
            ).wait_recv()
        f_copy(core, layer).start()

    contract = (((1,), (1,)), ((), ()))

    def inner_product(left, right):
        return lax.dot_general(left, right, contract, preferred_element_type=jnp.float32)

    def particles(kind, first, size, field):
        return mbuf[kind, first:first + size, :, field].reshape(size * slab, half)

    def gram(left, right):
        total = jnp.zeros((left[1] * slab, right[1] * slab), jnp.float32)
        for kind in range(2):
            for field in range(fields):
                total += inner_product(
                    particles(kind, *left, field), particles(kind, *right, field)
                )
        return total

    def squares(first, size):
        total = jnp.zeros((size * slab, half), jnp.float32)
        for kind in range(2):
            for field in range(fields):
                wide = particles(kind, first, size, field).astype(jnp.float32)
                total += wide * wide
        ones = jnp.ones((8, half), jnp.bfloat16)
        upper = total.astype(jnp.bfloat16)
        rest = total - upper.astype(jnp.float32)
        middle = rest.astype(jnp.bfloat16)
        lower = (rest - middle.astype(jnp.float32)).astype(jnp.bfloat16)
        return (
            inner_product(ones, upper) + inner_product(ones, middle) + inner_product(ones, lower)
        )

    def rs_span(deep):
        return pl.ds(0, 8 + (2 if deep else 1) * strip)

    steps = [(dx, dy) for dx in range(group // 2) for dy in range(planes) if dx + dy]
    steps.sort(key=lambda step: -(step[0] > 0) - (step[1] > 0))

    def chip_at(k, sign):
        dx, dy = steps[k - 1]
        columns = group // 2
        return (g // 2 + columns + sign * dx) % columns * planes + (y + planes + sign * dy) % planes

    def rs_copy(slot, k, deep):
        to = chip_at(k, 1)
        span = rs_span(deep)
        return remote(
            part.at[slot, to, span], inbox.at[slot, chip, span], rs_send.at[slot, k],
            rs_recv.at[slot, chip], at_chip(z, to, core),
        )

    def share(slot, total, norms, deep):
        for q in range(chips):
            first = total[q * strip:(q + 1) * strip]
            second = total[slab + q * strip:slab + (q + 1) * strip]
            part[slot, q, :8] = norms
            if deep:
                part[slot, q, 8:8 + strip] = first
                part[slot, q, 8 + strip:] = second
            else:
                part[slot, q, 8:8 + strip] = jnp.concatenate((first, second), axis=1)
        for k in range(1, chips):
            rs_copy(slot, k, deep).start()

    def collect(slot, deep):
        span = slice(0, 8 + (2 if deep else 1) * strip)
        total = part[slot, chip, span]
        for k in range(1, chips):
            source = chip_at(k, -1)
            remote(
                part.at[slot, chip, rs_span(deep)], inbox.at[slot, source, rs_span(deep)],
                rs_send.at[slot, k], rs_recv.at[slot, source], at_chip(z, source, core),
            ).wait_recv()
            total = total + inbox[slot, source, span]
        return total

    def swap(layer, source):
        return remote(
            swap_out.at[layer], swap_in.at[source], s_send.at[layer], s_recv.at[source],
            at(layer, g),
        )

    def swap_go(layer):
        if layer in (0, layers - 1):
            swap(layer, near).start()
        else:
            pl.when(z != layer)(lambda: swap(layer, near).start())

    def swap_rows(layer, total, row):
        swap_out[layer, :8] = total[:8]
        swap_out[layer, 8:] = total[8 + row * strip:8 + (row + 1) * strip]
        swap_go(layer)

    moves = [
        (dx, dy, dc)
        for dx in range(group // 2) for dy in range(planes) for dc in range(2) if dx + dy + dc
    ]
    moves.sort(key=lambda move: (-(move[0] > 0) - (move[1] > 0), -move[0], move[2]))

    def k_copy(k):
        dx, dy, dc = moves[k]
        to = (g // 2 + dx) % (group // 2) * 2 + (core + dc) % 2
        return remote(
            krow, kin.at[core, chip], k_send.at[k], k_recv.at[core, chip],
            (z * group + to, (y + dy) % planes),
        )

    def k_spread(verb):
        for k in range(peers - 1):
            getattr(k_copy(k), verb)()

    def k_rows(total):
        lanes = lax.broadcasted_iota(jnp.int32, (strip, pair), 1)
        local = lax.broadcasted_iota(jnp.int32, (strip, pair), 0) + chip * strip
        norms = total[0:1]
        first = jnp.sum(jnp.where(lanes == local, norms, 0.0), axis=1, keepdims=True)
        second = jnp.sum(jnp.where(lanes == local + slab, norms, 0.0), axis=1, keepdims=True)
        tall = both(odd, near == 1)
        left = lanes < slab
        upper = z % 2 == 1
        pick = jnp.where(tall, left.astype(jnp.int32), jnp.where(upper, 0, 1))
        own = jnp.where(pick == 1, first, second)
        others = total[4:5]
        distance = own + others - 2.0 * total[8:]
        divisor = jnp.full(distance.shape, scale * total_cells, jnp.float32)
        krow[...] = jnp.exp(-distance / divisor).astype(jnp.bfloat16)
        k_spread("start")
        kin[core, chip] = krow[...]

    m_ready(0, 1)
    m_hop(0, 1).start()

    @pl.when(inner)
    def _():
        for s in range(chunks):
            own_ready(s, 1, 2)
            z_half(s, 0).start()

    for k in range(2, group):
        m_ready(0, k)
        m_hop(0, k).start()

    @pl.when(is_end)
    def _():
        for k in range(1, group):
            m_ready(1, k)
            m_hop(1, k).start()

    @pl.when(inner)
    def _():
        for k in range(1, group):
            m_ready(1, k)
        m_own(1).wait()
        f_copy(core, z).start()
        for s in range(chunks):
            own_ready(s, 2)
            z_half(s, 1).start()
        z_copy(0, z, 0).start()
        z_copy(1, z, 0).start()
        z_copy(2, z, 0).start()
        z_copy(3, z, 0).start()
        m_wait(mate)
        m_wait(0)
        for layer in range(layers - 1):
            f_copy(1 - core, layer).wait_recv()

        @pl.when(even)
        def _():
            share(0, gram((0, 2), (0, 2)), squares(0, 2), True)

        @pl.when(odd)
        def _():
            norms = jnp.concatenate(
                (squares(0, 2)[:4], jnp.concatenate((squares(2, 1)[:4],) * 2, axis=1)), axis=0
            )
            share(0, gram((0, 2), (2, 1)), norms, False)

        pass_on(0, mate, 1)
        m_wait(layers - 1)
        f_copy(1 - core, layers - 1).wait_recv()

        @pl.when(even)
        def _():
            share(1, gram((2, 2), (2, 2)), squares(2, 2), True)

        @pl.when(odd)
        def _():
            norms = jnp.concatenate(
                (part[0, 0, :4], jnp.concatenate((squares(3, 1)[:4],) * 2, axis=1)), axis=0
            )
            share(1, gram((0, 2), (3, 1)), norms, False)

        pass_on(0, tip, 0)
        pass_on(1, tip, 0)
        pass_on(1, mate, 1)
        pass_on(2, mate, 1)
        pass_on(3, mate, 1)
        @pl.when(even)
        def _():
            total = collect(0, True)
            swap_rows(0, total, 0)
            swap_rows(1, total, 1)

        @pl.when(odd)
        def _():
            swap_out[2] = collect(0, False)
            swap_go(2)

        decode(0, z)
        decode(1, z)
        decode(2, z)
        decode(3, z)

        @pl.when(even)
        def _():
            total = collect(1, True)
            swap_rows(3, total, 1)
            swap_rows(2, total, 0)

        @pl.when(odd)
        def _():
            third = swap_out[2]
            fourth = collect(1, False)
            for layer in range(2):
                span = slice(layer * slab, (layer + 1) * slab)
                swap_out[layer, :4] = third[:4]
                swap_out[layer, 4:8] = jnp.concatenate(
                    (third[4:8, :slab], fourth[4:8, :slab]), axis=1
                )
                swap_out[layer, 8:] = jnp.concatenate((third[8:, span], fourth[8:, span]), axis=1)
                swap_go(layer)
            swap_out[3] = fourth
            swap_go(3)

        pass_on(2, tip, 0)
        pass_on(3, tip, 0)
        pass_on(0, far_tip, 1)
        pass_on(1, far_tip, 1)
        decode(0, tip)
        decode(1, tip)
        decode(2, tip)
        decode(3, tip)
        swap(mate, far).wait_recv()
        k_rows(swap_out[z] + swap_in[far])
        pass_on(2, far_tip, 1)
        pass_on(3, far_tip, 1)
        decode(0, mate)
        decode(1, mate)
        decode(2, mate)
        decode(3, mate)
        decode(0, far_tip)
        decode(1, far_tip)
        decode(2, far_tip)
        decode(3, far_tip)

    @pl.when(is_end)
    def _():
        m_own(1).wait()
        for s in range(chunks):
            own_ready(s)
            z_copy(s, z, 0).start()
        for s in range(chunks):
            decode(s, z)
        for layer in (toward, layers - 1 - toward):
            for s in range(chunks):
                z_copy(s, layer, 0).wait_recv()
                decode(s, layer)
        swap(toward, near).wait_recv()
        swap(mate, far).wait_recv()
        k_rows(swap_in[0] + swap_in[1])
        for s in range(2):
            z_copy(s, mate, 0).wait_recv()
            decode(s, mate)

    def k_ready(kind, k):
        q = (chip + k) % chips
        remote(
            krow, kin.at[kind, q], k_send.at[0], k_recv.at[kind, q], at(z, back(1))
        ).wait_recv()

    k_ready(1 - core, 0)
    for k in range(1, chips):
        k_ready(0, k)
        k_ready(1, k)

    @pl.when(near == 0)
    def _():
        kfull[:, :pair] = kin[0].reshape(slab, pair)
        kfull[:, pair:] = kin[1].reshape(slab, pair)

    @pl.when(near == 1)
    def _():
        kfull[:, pair:] = kin[0].reshape(slab, pair)
        tall = kin[1].reshape(slab, pair).astype(jnp.float32)
        kfull[:, :slab] = tall[:, :slab].T.astype(jnp.bfloat16)
        kfull[:, slab:pair] = tall[:, slab:].T.astype(jnp.bfloat16)

    rowsum = jnp.sum(kfull[...].astype(jnp.float32), axis=1, keepdims=True)
    pull = 2.0 / jnp.full((slab, 1), scale, jnp.float32) * rowsum
    m_own(0).wait()

    def o_own(s):
        span = pl.ds(pl.multiple_of(g * cells + s % 2 * half, 128), half)
        return pltpu.make_async_copy(
            outbox.at[s, g], out_ref.at[s // 2, :, span], own_sem.at[s]
        )

    def o_copy(s, k):
        field, side = s // 2, s % 2
        to = ring(k)
        span = pl.ds(pl.multiple_of(g * cells + side * half, 128), half)
        return remote(
            outbox.at[s, to], out_ref.at[field, :, span], o_send.at[s, k], o_recv.at[s, g],
            at(z, to),
        )

    for s in range(chunks):
        field, side = s // 2, s % 2

        if s >= 2:
            @pl.when(is_end)
            def _():
                z_copy(s, mate, 0).wait_recv()
                decode(s, mate)

        kernel = kfull[...]
        update = jnp.dot(
            kernel, high[s].reshape(count, half), preferred_element_type=jnp.float32
        ) + jnp.dot(kernel, low[s].reshape(count, half), preferred_element_type=jnp.float32)
        own = jnp.where(near == side, mbuf[core, z, :, field], mst[:, field])
        own = own.reshape(slab, half).astype(jnp.float32)
        update = update * (1.0 / LIFT) + pull * own
        square = update * update
        update = square * square * square * update * jnp.abs(update)
        outbox[s] = update.astype(jnp.bfloat16).reshape(group, rows, half)
        for k in (2, 3, 1):
            o_copy(s, k).start()
        o_own(s).start()

    for k in range(1, group):
        m_copy(0, k).wait_send()
        m_copy(1, k).wait_send()
    for k in range(group):
        m_hop(0, k).wait_send()

    @pl.when(is_end)
    def _():
        for k in range(group):
            m_hop(1, k).wait_send()
    for s in range(chunks):
        for k in range(1, group):
            a_copy(s, k).wait_send()
        z_copy(s, z, 0).wait_send()

    @pl.when(inner)
    def _():
        for layer in range(layers):
            f_copy(core, layer).wait_send()
        for s in range(chunks):
            z_half(s, 0).wait_send()
            z_half(s, 1).wait_send()
            z_copy(s, tip, 0).wait_send()
            z_copy(s, mate, 1).wait_send()
            z_copy(s, far_tip, 1).wait_send()
        for slot in range(2):
            for k in range(1, chips):
                @pl.when(even)
                def _():
                    rs_copy(slot, k, True).wait_send()

                @pl.when(odd)
                def _():
                    rs_copy(slot, k, False).wait_send()

        swap(0, near).wait_send()
        swap(layers - 1, near).wait_send()
        swap(mate, near).wait_send()

    k_spread("wait_send")

    for s in range(chunks):
        field, side = s // 2, s % 2
        o_own(s).wait()
        for k in range(1, group):
            o_copy(s, k).wait_send()
            source = back(k)
            span = pl.ds(pl.multiple_of(source * cells + side * half, 128), half)
            remote(
                outbox.at[s, source], out_ref.at[field, :, span], o_send.at[s, k],
                o_recv.at[s, source], at(z, source),
            ).wait_recv()


def expand_kernel(factor, code_ref, out_ref):
    wide = code_ref[...].astype(jnp.float32)
    root = jnp.exp2(jnp.log2(jnp.abs(wide)) * 0.125) * factor
    out_ref[...] = jnp.where(wide < 0.0, -root, root)


def fused_body(layers, group, planes, models, gradients, length_scale):
    fields, rows, width = models.shape
    cells = width // group
    half = cells // 2
    slab = group * rows
    count = layers * slab
    chips = group // 2 * planes
    strip = slab // chips
    chunks = fields * 2
    pair = 2 * slab
    peers = group * planes
    dma = pltpu.SemaphoreType.DMA
    vmem = pltpu.VMEM
    gathered = pl.pallas_call(
        functools.partial(stein_kernel, layers, group, planes),
        out_shape=jax.ShapeDtypeStruct(models.shape, jnp.bfloat16),
        in_specs=[
            pl.BlockSpec(memory_space=pltpu.SMEM),
            pl.BlockSpec(memory_space=pl.ANY),
            pl.BlockSpec(memory_space=pl.ANY),
        ],
        out_specs=pl.BlockSpec(memory_space=pl.ANY),
        scratch_shapes=[
            vmem(models.shape, jnp.bfloat16),
            vmem(models.shape, jnp.bfloat16),
            vmem((chunks, group, rows, half), jnp.bfloat16),
            vmem((group, fields, rows, half), jnp.bfloat16),
            vmem((2, layers, group, fields, rows, half), jnp.bfloat16),
            vmem((chunks, layers, group, rows, half), jnp.bfloat16),
            vmem((chunks, layers, slab, half), jnp.bfloat16),
            vmem((chunks, layers, slab, half), jnp.bfloat16),
            vmem((2, chips, 8 + 2 * strip, pair), jnp.float32),
            vmem((2, chips, 8 + 2 * strip, pair), jnp.float32),
            vmem((layers, 8 + strip, pair), jnp.float32),
            vmem((2, 8 + strip, pair), jnp.float32),
            vmem((strip, pair), jnp.bfloat16),
            vmem((2, chips, strip, pair), jnp.bfloat16),
            vmem((slab, count), jnp.bfloat16),
            vmem((chunks, group, rows, half), jnp.bfloat16),
            dma((chunks,)),
            dma((2, chunks)),
            dma((4,)),
            dma((2, group)),
            dma((2, group)),
            dma((2, group)),
            dma((layers, group)),
            dma((layers,)),
            dma((layers,)),
            dma((chunks, group)),
            dma((chunks, group)),
            dma((2, chunks, layers)),
            dma((chunks, layers)),
            dma((2, chips)),
            dma((2, chips)),
            dma((layers,)),
            dma((2,)),
            dma((peers,)),
            dma((2, chips)),
            dma((chunks, group)),
            dma((chunks, group)),
        ],
        compiler_params=pltpu.CompilerParams(collective_id=0, has_side_effects=True),
        name="stein",
    )(length_scale, models, gradients)
    return pl.pallas_call(
        functools.partial(expand_kernel, 1.0 / count),
        out_shape=jax.ShapeDtypeStruct(models.shape, jnp.float32),
        grid=(fields,),
        in_specs=[pl.BlockSpec((1, rows, width), lambda i: (i, 0, 0))],
        out_specs=pl.BlockSpec((1, rows, width), lambda i: (i, 0, 0)),
        name="expand",
    )(gathered)


def solution(mesh):
    spread, planes = mesh.shape["dom"], mesh.shape["cell"]
    layers = math.isqrt(spread)
    group = spread // layers

    def body(models, gradients, length_scale):
        _, rows, width = models.shape
        slab = group * rows
        chips = group // 2 * planes
        fits = (
            layers == 4
            and group == 4
            and models.shape[0] == 2
            and layers * group == spread
            and width % (group * 256) == 0
            and rows % 16 == 0
            and slab % 128 == 0
            and slab % (chips * 16) == 0
        )
        if not fits:
            return plain_body(models, gradients, length_scale)
        return fused_body(layers, group, planes, models, gradients, length_scale)

    placed = (P(None, "dom", "cell"), P(None, "dom", "cell"), P())
    return jax.shard_map(
        body, mesh=mesh, in_specs=placed, out_specs=P(None, "dom", "cell"), check_vma=False
    )
```

```python
import functools
import math

import jax
import jax.numpy as jnp
from jax import lax
from jax.experimental import pallas as pl
from jax.experimental.pallas import tpu as pltpu
from jax.sharding import PartitionSpec as P

MESH = pl.DeviceIdType.MESH


def plain_body(models, gradients, length_scale):
    local_models, local_grads = (
        lax.all_to_all(models, "dom", split_axis=2, concat_axis=1, tiled=True),
        lax.all_to_all(gradients, "dom", split_axis=2, concat_axis=1, tiled=True),
    )
    cell_block = local_models.shape[2]
    particles = local_models.shape[1]
    cell_count = cell_block * lax.axis_size("dom") * lax.axis_size("cell")
    scale_value = length_scale[0]
    divisor = scale_value * cell_count
    partial_value = jnp.einsum(
        "kpc,kqc->pq", local_models, local_models, preferred_element_type=jnp.float32
    )
    summed = lax.psum(partial_value, "cell")
    row_block = lax.psum_scatter(summed, "dom", scatter_dimension=0, tiled=True)
    row_count = row_block.shape[0]
    row_start = lax.axis_index("dom") * row_count
    own_squares = jnp.diagonal(lax.dynamic_slice_in_dim(row_block, row_start, row_count, 1))
    squares = lax.all_gather(own_squares, "dom", axis=0, tiled=True)
    distance = own_squares[:, None] + squares[None, :] - 2.0 * row_block
    kernel = lax.all_gather(
        jnp.exp(-distance / divisor).astype(jnp.bfloat16), "dom", axis=0, tiled=True
    )
    rowsum = jnp.sum(kernel.astype(jnp.float32), axis=1)
    stacked = jnp.concatenate((local_grads, local_models), axis=2)
    product = jnp.einsum("pq,kqc->kpc", kernel, stacked, preferred_element_type=jnp.float32)
    attract = product[:, :, :cell_block]
    pulled = product[:, :, cell_block:]
    update = (
        attract
        + 2.0 / scale_value * (rowsum[None, :, None] * local_models.astype(jnp.float32) - pulled)
    ) / particles
    return lax.all_to_all(update, "dom", split_axis=1, concat_axis=2, tiled=True)


LIFT = 512.0


def stein_kernel(
    layers, group, planes,
    scale_ref, models_ref, grads_ref, out_ref,
    m_loc, g_loc, code, mst, mbuf, hbuf, high, low, part, inbox, swap_out, swap_in,
    krow, kin, kfull, outbox,
    ready, d_send, own_sem, h_send, loc_sem, m_send, m_recv, mz_send, mz_recv, f_send, f_recv, a_send, a_recv, z_send, z_recv,
    rs_send, rs_recv, s_send, s_recv, k_send, k_recv, o_send, o_recv,
):
    fields, rows, width = models_ref.shape
    cells = width // group
    half = cells // 2
    slab = group * rows
    count = layers * slab
    chips = group // 2 * planes
    peers = group * planes
    strip = slab // chips
    chunks = fields * 2
    pair = 2 * slab
    total_cells = width * planes
    dom = lax.axis_index("dom")
    y = lax.axis_index("cell")
    z = dom // group
    g = dom % group
    core = g % 2
    chip = g // 2 * planes + y
    near = z // 2
    far = 1 - near
    inner = jnp.logical_and(z > 0, z < layers - 1)
    is_end = jnp.logical_not(inner)
    mate = layers - 1 - z
    tip = near * (layers - 1)
    far_tip = far * (layers - 1)
    toward = jnp.where(inner, mate, 1 + near)
    even = core == 0
    odd = core == 1

    def both(left, right):
        return jnp.logical_and(left, right)

    def at(layer, which):
        return (layer * group + which, y)

    def at_chip(layer, which, kind):
        return (layer * group + which // planes * 2 + kind, which % planes)

    def ring(k):
        return (g, g + 1 - 2 * core, (g + 2) % group, group - 1 - g)[k]

    back = ring

    def remote(src, dst, send, recv, device):
        return pltpu.make_async_remote_copy(
            src_ref=src, dst_ref=dst, send_sem=send, recv_sem=recv,
            device_id=device, device_id_type=MESH,
        )

    loads = [
        pltpu.make_async_copy(models_ref, m_loc, loc_sem.at[0]),
        pltpu.make_async_copy(grads_ref, g_loc, loc_sem.at[1]),
    ]
    for copy in loads:
        copy.start()

    barrier = pltpu.get_barrier_semaphore()
    here = g * planes + y

    def greet(k, carry):
        to = (here + k) % peers
        pl.semaphore_signal(
            barrier, inc=1, device_id=(z * group + to // planes, to % planes), device_id_type=MESH
        )
        return carry

    lax.fori_loop(1, peers, greet, 0)
    pl.semaphore_signal(barrier, inc=1, device_id=at(toward, g), device_id_type=MESH)

    @pl.when(inner)
    def _():
        pl.semaphore_signal(barrier, inc=1, device_id=at(tip, g), device_id_type=MESH)

    @pl.when(z == 1)
    def _():
        pl.semaphore_signal(barrier, inc=1, device_id=at(far_tip, g), device_id_type=MESH)

    pl.semaphore_wait(barrier, peers + jnp.where(z > 0, 1, 0))

    @pl.when(z == 1)
    def _():
        pl.semaphore_signal(ready, inc=1, device_id=at(tip, g), device_id_type=MESH)
        pl.semaphore_signal(ready, inc=1, device_id=at(mate, g), device_id_type=MESH)

    @pl.when(z == 0)
    def _():
        pl.semaphore_signal(ready, inc=1, device_id=at(1, g), device_id_type=MESH)

    def m_part(side, to):
        return models_ref.at[:, :, pl.ds(pl.multiple_of(to * cells + side * half, 128), half)]

    sides = (jnp.where(z == 0, near, far), jnp.where(z == 0, far, near))

    def landing(slot, kind, source):
        return mbuf.at[kind, z, source] if slot else mst.at[source]

    def m_copy(slot, k):
        to = ring(k)
        return remote(
            m_part(sides[slot], to), landing(slot, to % 2, g),
            m_send.at[slot, k], m_recv.at[slot, g], at(z, to),
        )

    def m_own(slot):
        return pltpu.make_async_copy(
            m_part(sides[slot], g), landing(slot, core, g), loc_sem.at[2 + slot]
        )

    def m_hop(slot, k):
        source = back(k)
        src = m_part(sides[slot], g) if k == 0 else landing(slot, core, source)
        return remote(
            src, mbuf.at[core, z, source], mz_send.at[slot, k], mz_recv.at[z, source],
            at(1 + sides[slot], g),
        )

    def m_ready(slot, k):
        source = back(k)
        remote(
            m_part(sides[slot], g), landing(slot, core, source),
            m_send.at[slot, k], m_recv.at[slot, source], at(z, source),
        ).wait_recv()

    for slot in range(2):
        for k in range(1, group):
            m_copy(slot, k).start()
        m_own(slot).start()

    @pl.when(z == layers - 1)
    def _():
        m_hop(1, 0).start()

    m_hop(0, 0).start()

    for copy in loads:
        copy.wait()

    scale = scale_ref[0]

    def a_copy(s, k):
        to = ring(k)
        return remote(
            code.at[s, to], hbuf.at[s, z, g], a_send.at[s, k], a_recv.at[s, g], at(z, to)
        )

    weight = 2.0 * LIFT / jnp.full((rows, half), scale, jnp.float32)
    for s in range(chunks):
        field, side = s // 2, s % 2
        for to in range(group):
            span = slice(to * cells + side * half, to * cells + side * half + half)
            value = g_loc[field, :, span].astype(jnp.float32) * LIFT
            value = value - weight * m_loc[field, :, span].astype(jnp.float32)
            square = value * value
            code[s, to] = (square * square * square * value * jnp.abs(value)).astype(jnp.bfloat16)
        for k in range(1, group):
            a_copy(s, k).start()
        hbuf[s, z, g] = code[s, g]

    def z_copy(s, layer, outward):
        block = hbuf.at[s, layer]
        return remote(
            block, block, z_send.at[outward, s, layer], z_recv.at[s, layer],
            at(tip if outward else toward, g),
        )

    def decode(s, layer):
        value = hbuf[s, layer].reshape(slab, half).astype(jnp.float32)
        root = jnp.exp2(jnp.log2(jnp.abs(value)) * 0.125)
        root = jnp.where(value < 0.0, -root, root)
        upper = root.astype(jnp.bfloat16)
        high[s, layer] = upper
        low[s, layer] = (root - upper.astype(jnp.float32)).astype(jnp.bfloat16)

    def own_ready(s, first=1, last=group):
        for k in range(first, last):
            source = back(k)
            remote(
                code.at[s, g], hbuf.at[s, z, source], a_send.at[s, k], a_recv.at[s, source],
                at(z, source),
            ).wait_recv()

    def z_half(s, side):
        start = (g // 2 + side) % 2 * 2
        block = hbuf.at[s, z, pl.ds(start, 2)]
        return remote(block, block, h_send.at[side, s], z_recv.at[s, z], at(tip, g))

    def z_direct(s, k):
        to = ring(k)
        return remote(
            code.at[s, to], hbuf.at[s, z, g], d_send.at[s, k], z_recv.at[s, z],
            at(jnp.where(z == 1, tip, mate), to),
        )

    def pass_on(s, layer, outward):
        z_copy(s, layer, outward).wait_recv()
        z_copy(s, layer, outward).start()

    def f_copy(kind, layer):
        block = mbuf.at[kind, layer]
        return remote(
            block, block, f_send.at[layer], f_recv.at[layer], at(z, g + 1 - 2 * core)
        )

    def m_wait(layer):
        for k in range(group):
            source = back(k)
            remote(
                m_part(near, g), mbuf.at[core, layer, source], mz_send.at[0, k],
                mz_recv.at[layer, source], at(layer, g),
            ).wait_recv()
        f_copy(core, layer).start()

    contract = (((1,), (1,)), ((), ()))

    def inner_product(left, right):
        return lax.dot_general(left, right, contract, preferred_element_type=jnp.float32)

    def particles(kind, first, size, field):
        return mbuf[kind, first:first + size, :, field].reshape(size * slab, half)

    def gram(left, right):
        total = jnp.zeros((left[1] * slab, right[1] * slab), jnp.float32)
        for kind in range(2):
            for field in range(fields):
                total += inner_product(
                    particles(kind, *left, field), particles(kind, *right, field)
                )
        return total

    def squares(first, size):
        total = jnp.zeros((size * slab, half), jnp.float32)
        for kind in range(2):
            for field in range(fields):
                wide = particles(kind, first, size, field).astype(jnp.float32)
                total += wide * wide
        ones = jnp.ones((8, half), jnp.bfloat16)
        upper = total.astype(jnp.bfloat16)
        rest = total - upper.astype(jnp.float32)
        middle = rest.astype(jnp.bfloat16)
        lower = (rest - middle.astype(jnp.float32)).astype(jnp.bfloat16)
        return (
            inner_product(ones, upper) + inner_product(ones, middle) + inner_product(ones, lower)
        )

    def rs_span(deep):
        return pl.ds(0, 8 + (2 if deep else 1) * strip)

    steps = [(dx, dy) for dx in range(group // 2) for dy in range(planes) if dx + dy]
    steps.sort(key=lambda step: -(step[0] > 0) - (step[1] > 0))

    def chip_at(k, sign):
        dx, dy = steps[k - 1]
        columns = group // 2
        return (g // 2 + columns + sign * dx) % columns * planes + (y + planes + sign * dy) % planes

    def rs_copy(slot, k, deep):
        to = chip_at(k, 1)
        span = rs_span(deep)
        return remote(
            part.at[slot, to, span], inbox.at[slot, chip, span], rs_send.at[slot, k],
            rs_recv.at[slot, chip], at_chip(z, to, core),
        )

    def share(slot, total, norms, deep):
        for q in range(chips):
            first = total[q * strip:(q + 1) * strip]
            second = total[slab + q * strip:slab + (q + 1) * strip]
            part[slot, q, :8] = norms
            if deep:
                part[slot, q, 8:8 + strip] = first
                part[slot, q, 8 + strip:] = second
            else:
                part[slot, q, 8:8 + strip] = jnp.concatenate((first, second), axis=1)
        for k in range(1, chips):
            rs_copy(slot, k, deep).start()

    def collect(slot, deep):
        span = slice(0, 8 + (2 if deep else 1) * strip)
        total = part[slot, chip, span]
        for k in range(1, chips):
            source = chip_at(k, -1)
            remote(
                part.at[slot, chip, rs_span(deep)], inbox.at[slot, source, rs_span(deep)],
                rs_send.at[slot, k], rs_recv.at[slot, source], at_chip(z, source, core),
            ).wait_recv()
            total = total + inbox[slot, source, span]
        return total

    def swap(layer, source):
        return remote(
            swap_out.at[layer], swap_in.at[source], s_send.at[layer], s_recv.at[source],
            at(layer, g),
        )

    def swap_go(layer):
        if layer in (0, layers - 1):
            swap(layer, near).start()
        else:
            pl.when(z != layer)(lambda: swap(layer, near).start())

    def swap_rows(layer, total, row):
        swap_out[layer, :8] = total[:8]
        swap_out[layer, 8:] = total[8 + row * strip:8 + (row + 1) * strip]
        swap_go(layer)

    moves = [
        (dx, dy, dc)
        for dx in range(group // 2) for dy in range(planes) for dc in range(2) if dx + dy + dc
    ]
    moves.sort(key=lambda move: (-(move[0] > 0) - (move[1] > 0), -move[0], move[2]))

    def k_copy(k):
        dx, dy, dc = moves[k]
        to = (g // 2 + dx) % (group // 2) * 2 + (core + dc) % 2
        return remote(
            krow, kin.at[core, chip], k_send.at[k], k_recv.at[core, chip],
            (z * group + to, (y + dy) % planes),
        )

    def k_spread(verb):
        for k in range(peers - 1):
            getattr(k_copy(k), verb)()

    def k_rows(total):
        lanes = lax.broadcasted_iota(jnp.int32, (strip, pair), 1)
        local = lax.broadcasted_iota(jnp.int32, (strip, pair), 0) + chip * strip
        norms = total[0:1]
        first = jnp.sum(jnp.where(lanes == local, norms, 0.0), axis=1, keepdims=True)
        second = jnp.sum(jnp.where(lanes == local + slab, norms, 0.0), axis=1, keepdims=True)
        tall = both(odd, near == 1)
        left = lanes < slab
        upper = z % 2 == 1
        pick = jnp.where(tall, left.astype(jnp.int32), jnp.where(upper, 0, 1))
        own = jnp.where(pick == 1, first, second)
        others = total[4:5]
        distance = own + others - 2.0 * total[8:]
        divisor = jnp.full(distance.shape, scale * total_cells, jnp.float32)
        krow[...] = jnp.exp(-distance / divisor).astype(jnp.bfloat16)
        k_spread("start")
        kin[core, chip] = krow[...]

    @pl.when(z == 0)
    def _():
        pl.semaphore_wait(ready, 1)
        m_hop(1, 0).start()

    m_ready(0, 1)
    m_hop(0, 1).start()

    @pl.when(is_end)
    def _():
        m_ready(1, 1)
        m_hop(1, 1).start()

    @pl.when(inner)
    def _():
        @pl.when(z == 1)
        def _():
            pl.semaphore_wait(ready, 1)
            for s in range(chunks):
                for k in (0, 1, 2, 3):
                    z_direct(s, k).start()

        @pl.when(z != 1)
        def _():
            for s in range(chunks):
                own_ready(s, 1, 2)
                z_half(s, 0).start()

    for k in range(2, group):
        m_ready(0, k)
        m_hop(0, k).start()

    @pl.when(z == 2)
    def _():
        pl.semaphore_wait(ready, 1)
        for s in range(chunks):
            for k in range(group):
                z_direct(s, k).start()

    @pl.when(is_end)
    def _():
        for k in range(2, group):
            m_ready(1, k)
            m_hop(1, k).start()

    @pl.when(inner)
    def _():
        for k in range(1, group):
            m_ready(1, k)
        m_own(1).wait()
        f_copy(core, z).start()
        for s in range(chunks):
            pl.when(z == 1)(lambda: own_ready(s, 1, 2))
            own_ready(s, 2)

            @pl.when(z != 1)
            def _():
                z_half(s, 1).start()
        pl.when(z != 2)(z_copy(0, z, 0).start)
        pl.when(z != 2)(z_copy(1, z, 0).start)
        pl.when(z != 2)(z_copy(2, z, 0).start)
        pl.when(z != 2)(z_copy(3, z, 0).start)
        m_wait(mate)
        m_wait(0)
        for layer in range(layers - 1):
            f_copy(1 - core, layer).wait_recv()

        @pl.when(even)
        def _():
            share(0, gram((0, 2), (0, 2)), squares(0, 2), True)

        @pl.when(odd)
        def _():
            norms = jnp.concatenate(
                (squares(0, 2)[:4], jnp.concatenate((squares(2, 1)[:4],) * 2, axis=1)), axis=0
            )
            share(0, gram((0, 2), (2, 1)), norms, False)

        pass_on(0, mate, 1)
        m_wait(layers - 1)
        f_copy(1 - core, layers - 1).wait_recv()

        @pl.when(even)
        def _():
            share(1, gram((2, 2), (2, 2)), squares(2, 2), True)

        @pl.when(odd)
        def _():
            norms = jnp.concatenate(
                (part[0, 0, :4], jnp.concatenate((squares(3, 1)[:4],) * 2, axis=1)), axis=0
            )
            share(1, gram((0, 2), (3, 1)), norms, False)

        pass_on(0, tip, 0)
        pass_on(1, tip, 0)
        pass_on(1, mate, 1)
        pass_on(2, mate, 1)
        pass_on(3, mate, 1)
        @pl.when(even)
        def _():
            total = collect(0, True)
            swap_rows(0, total, 0)
            swap_rows(1, total, 1)

        @pl.when(odd)
        def _():
            swap_out[2] = collect(0, False)
            swap_go(2)

        decode(0, z)
        decode(1, z)
        decode(2, z)
        decode(3, z)

        @pl.when(even)
        def _():
            total = collect(1, True)
            swap_rows(3, total, 1)
            swap_rows(2, total, 0)

        @pl.when(odd)
        def _():
            third = swap_out[2]
            fourth = collect(1, False)
            for layer in range(2):
                span = slice(layer * slab, (layer + 1) * slab)
                swap_out[layer, :4] = third[:4]
                swap_out[layer, 4:8] = jnp.concatenate(
                    (third[4:8, :slab], fourth[4:8, :slab]), axis=1
                )
                swap_out[layer, 8:] = jnp.concatenate((third[8:, span], fourth[8:, span]), axis=1)
                swap_go(layer)
            swap_out[3] = fourth
            swap_go(3)

        pass_on(2, tip, 0)
        pass_on(3, tip, 0)
        pass_on(0, far_tip, 1)
        pass_on(1, far_tip, 1)
        decode(0, tip)
        decode(1, tip)
        decode(2, tip)
        decode(3, tip)
        swap(mate, far).wait_recv()
        k_rows(swap_out[z] + swap_in[far])
        pass_on(2, far_tip, 1)
        pass_on(3, far_tip, 1)
        decode(0, mate)
        decode(1, mate)
        decode(2, mate)
        decode(3, mate)
        decode(0, far_tip)
        decode(1, far_tip)
        decode(2, far_tip)
        decode(3, far_tip)

    @pl.when(is_end)
    def _():
        m_own(1).wait()
        for s in range(chunks):
            own_ready(s)
            z_copy(s, z, 0).start()
        for s in range(chunks):
            decode(s, z)
        for layer in (toward, layers - 1 - toward):
            for s in range(chunks):
                z_copy(s, layer, 0).wait_recv()
                decode(s, layer)
        swap(toward, near).wait_recv()
        swap(mate, far).wait_recv()
        k_rows(swap_in[0] + swap_in[1])
        for s in range(2):
            z_copy(s, mate, 0).wait_recv()
            decode(s, mate)

    def k_ready(kind, k):
        q = (chip + k) % chips
        remote(
            krow, kin.at[kind, q], k_send.at[0], k_recv.at[kind, q], at(z, back(1))
        ).wait_recv()

    k_ready(1 - core, 0)
    for k in range(1, chips):
        k_ready(0, k)
        k_ready(1, k)

    @pl.when(near == 0)
    def _():
        kfull[:, :pair] = kin[0].reshape(slab, pair)
        kfull[:, pair:] = kin[1].reshape(slab, pair)

    @pl.when(near == 1)
    def _():
        kfull[:, pair:] = kin[0].reshape(slab, pair)
        tall = kin[1].reshape(slab, pair).astype(jnp.float32)
        kfull[:, :slab] = tall[:, :slab].T.astype(jnp.bfloat16)
        kfull[:, slab:pair] = tall[:, slab:].T.astype(jnp.bfloat16)

    rowsum = jnp.sum(kfull[...].astype(jnp.float32), axis=1, keepdims=True)
    pull = 2.0 / jnp.full((slab, 1), scale, jnp.float32) * rowsum
    m_own(0).wait()

    def o_own(s):
        span = pl.ds(pl.multiple_of(g * cells + s % 2 * half, 128), half)
        return pltpu.make_async_copy(
            outbox.at[s, g], out_ref.at[s // 2, :, span], own_sem.at[s]
        )

    def o_copy(s, k):
        field, side = s // 2, s % 2
        to = ring(k)
        span = pl.ds(pl.multiple_of(g * cells + side * half, 128), half)
        return remote(
            outbox.at[s, to], out_ref.at[field, :, span], o_send.at[s, k], o_recv.at[s, g],
            at(z, to),
        )

    for s in range(chunks):
        field, side = s // 2, s % 2

        if s >= 2:
            @pl.when(is_end)
            def _():
                z_copy(s, mate, 0).wait_recv()
                decode(s, mate)

        kernel = kfull[...]
        update = jnp.dot(
            kernel, high[s].reshape(count, half), preferred_element_type=jnp.float32
        ) + jnp.dot(kernel, low[s].reshape(count, half), preferred_element_type=jnp.float32)
        own = jnp.where(sides[1] == side, mbuf[core, z, :, field], mst[:, field])
        own = own.reshape(slab, half).astype(jnp.float32)
        update = update * (1.0 / LIFT) + pull * own
        square = update * update
        update = square * square * square * update * jnp.abs(update)
        outbox[s] = update.astype(jnp.bfloat16).reshape(group, rows, half)
        for k in (2, 3, 1):
            o_copy(s, k).start()
        o_own(s).start()

    for k in range(1, group):
        m_copy(0, k).wait_send()
        m_copy(1, k).wait_send()
    for k in range(group):
        m_hop(0, k).wait_send()

    @pl.when(is_end)
    def _():
        for k in range(group):
            m_hop(1, k).wait_send()
    for s in range(chunks):
        for k in range(1, group):
            a_copy(s, k).wait_send()
        pl.when(z != 2)(z_copy(s, z, 0).wait_send)

    @pl.when(inner)
    def _():
        for layer in range(layers):
            f_copy(core, layer).wait_send()
        for s in range(chunks):
            for k in range(group):
                z_direct(s, k).wait_send()

            @pl.when(z != 1)
            def _():
                z_half(s, 0).wait_send()
                z_half(s, 1).wait_send()

            z_copy(s, tip, 0).wait_send()
            z_copy(s, mate, 1).wait_send()
            z_copy(s, far_tip, 1).wait_send()
        for slot in range(2):
            for k in range(1, chips):
                @pl.when(even)
                def _():
                    rs_copy(slot, k, True).wait_send()

                @pl.when(odd)
                def _():
                    rs_copy(slot, k, False).wait_send()

        swap(0, near).wait_send()
        swap(layers - 1, near).wait_send()
        swap(mate, near).wait_send()

    k_spread("wait_send")

    for s in range(chunks):
        field, side = s // 2, s % 2
        o_own(s).wait()
        for k in range(1, group):
            o_copy(s, k).wait_send()
            source = back(k)
            span = pl.ds(pl.multiple_of(source * cells + side * half, 128), half)
            remote(
                outbox.at[s, source], out_ref.at[field, :, span], o_send.at[s, k],
                o_recv.at[s, source], at(z, source),
            ).wait_recv()


def expand_kernel(factor, code_ref, out_ref):
    wide = code_ref[...].astype(jnp.float32)
    root = jnp.exp2(jnp.log2(jnp.abs(wide)) * 0.125) * factor
    out_ref[...] = jnp.where(wide < 0.0, -root, root)


def fused_body(layers, group, planes, models, gradients, length_scale):
    fields, rows, width = models.shape
    cells = width // group
    half = cells // 2
    slab = group * rows
    count = layers * slab
    chips = group // 2 * planes
    strip = slab // chips
    chunks = fields * 2
    pair = 2 * slab
    peers = group * planes
    dma = pltpu.SemaphoreType.DMA
    vmem = pltpu.VMEM
    gathered = pl.pallas_call(
        functools.partial(stein_kernel, layers, group, planes),
        out_shape=jax.ShapeDtypeStruct(models.shape, jnp.bfloat16),
        in_specs=[
            pl.BlockSpec(memory_space=pltpu.SMEM),
            pl.BlockSpec(memory_space=pl.ANY),
            pl.BlockSpec(memory_space=pl.ANY),
        ],
        out_specs=pl.BlockSpec(memory_space=pl.ANY),
        scratch_shapes=[
            vmem(models.shape, jnp.bfloat16),
            vmem(models.shape, jnp.bfloat16),
            vmem((chunks, group, rows, half), jnp.bfloat16),
            vmem((group, fields, rows, half), jnp.bfloat16),
            vmem((2, layers, group, fields, rows, half), jnp.bfloat16),
            vmem((chunks, layers, group, rows, half), jnp.bfloat16),
            vmem((chunks, layers, slab, half), jnp.bfloat16),
            vmem((chunks, layers, slab, half), jnp.bfloat16),
            vmem((2, chips, 8 + 2 * strip, pair), jnp.float32),
            vmem((2, chips, 8 + 2 * strip, pair), jnp.float32),
            vmem((layers, 8 + strip, pair), jnp.float32),
            vmem((2, 8 + strip, pair), jnp.float32),
            vmem((strip, pair), jnp.bfloat16),
            vmem((2, chips, strip, pair), jnp.bfloat16),
            vmem((slab, count), jnp.bfloat16),
            vmem((chunks, group, rows, half), jnp.bfloat16),
            pltpu.SemaphoreType.REGULAR,
            dma((chunks, group)),
            dma((chunks,)),
            dma((2, chunks)),
            dma((4,)),
            dma((2, group)),
            dma((2, group)),
            dma((2, group)),
            dma((layers, group)),
            dma((layers,)),
            dma((layers,)),
            dma((chunks, group)),
            dma((chunks, group)),
            dma((2, chunks, layers)),
            dma((chunks, layers)),
            dma((2, chips)),
            dma((2, chips)),
            dma((layers,)),
            dma((2,)),
            dma((peers,)),
            dma((2, chips)),
            dma((chunks, group)),
            dma((chunks, group)),
        ],
        compiler_params=pltpu.CompilerParams(collective_id=0, has_side_effects=True),
        name="stein",
    )(length_scale, models, gradients)
    return pl.pallas_call(
        functools.partial(expand_kernel, 1.0 / count),
        out_shape=jax.ShapeDtypeStruct(models.shape, jnp.float32),
        grid=(fields,),
        in_specs=[pl.BlockSpec((1, rows, width), lambda i: (i, 0, 0))],
        out_specs=pl.BlockSpec((1, rows, width), lambda i: (i, 0, 0)),
        name="expand",
    )(gathered)


def solution(mesh):
    spread, planes = mesh.shape["dom"], mesh.shape["cell"]
    layers = math.isqrt(spread)
    group = spread // layers

    def body(models, gradients, length_scale):
        _, rows, width = models.shape
        slab = group * rows
        chips = group // 2 * planes
        fits = (
            layers == 4
            and group == 4
            and models.shape[0] == 2
            and layers * group == spread
            and width % (group * 256) == 0
            and rows % 16 == 0
            and slab % 128 == 0
            and slab % (chips * 16) == 0
        )
        if not fits:
            return plain_body(models, gradients, length_scale)
        return fused_body(layers, group, planes, models, gradients, length_scale)

    placed = (P(None, "dom", "cell"), P(None, "dom", "cell"), P())
    return jax.shard_map(
        body, mesh=mesh, in_specs=placed, out_specs=P(None, "dom", "cell"), check_vma=False
    )
```

```python
import functools
import math

import jax
import jax.numpy as jnp
from jax import lax
from jax.experimental import pallas as pl
from jax.experimental.pallas import tpu as pltpu
from jax.sharding import PartitionSpec as P

MESH = pl.DeviceIdType.MESH


def plain_body(models, gradients, length_scale):
    local_models, local_grads = (
        lax.all_to_all(models, "dom", split_axis=2, concat_axis=1, tiled=True),
        lax.all_to_all(gradients, "dom", split_axis=2, concat_axis=1, tiled=True),
    )
    cell_block = local_models.shape[2]
    particles = local_models.shape[1]
    cell_count = cell_block * lax.axis_size("dom") * lax.axis_size("cell")
    scale_value = length_scale[0]
    divisor = scale_value * cell_count
    partial_value = jnp.einsum(
        "kpc,kqc->pq", local_models, local_models, preferred_element_type=jnp.float32
    )
    summed = lax.psum(partial_value, "cell")
    row_block = lax.psum_scatter(summed, "dom", scatter_dimension=0, tiled=True)
    row_count = row_block.shape[0]
    row_start = lax.axis_index("dom") * row_count
    own_squares = jnp.diagonal(lax.dynamic_slice_in_dim(row_block, row_start, row_count, 1))
    squares = lax.all_gather(own_squares, "dom", axis=0, tiled=True)
    distance = own_squares[:, None] + squares[None, :] - 2.0 * row_block
    kernel = lax.all_gather(
        jnp.exp(-distance / divisor).astype(jnp.bfloat16), "dom", axis=0, tiled=True
    )
    rowsum = jnp.sum(kernel.astype(jnp.float32), axis=1)
    stacked = jnp.concatenate((local_grads, local_models), axis=2)
    product = jnp.einsum("pq,kqc->kpc", kernel, stacked, preferred_element_type=jnp.float32)
    attract = product[:, :, :cell_block]
    pulled = product[:, :, cell_block:]
    update = (
        attract
        + 2.0 / scale_value * (rowsum[None, :, None] * local_models.astype(jnp.float32) - pulled)
    ) / particles
    return lax.all_to_all(update, "dom", split_axis=1, concat_axis=2, tiled=True)


LIFT = 512.0


def stein_kernel(
    layers, group, planes,
    scale_ref, models_ref, grads_ref, out_ref,
    m_loc, g_loc, code, mst, mbuf, hbuf, high, low, part, inbox, swap_out, swap_in,
    krow, kin, kfull, outbox,
    ready, d_send, own_sem, h_send, loc_sem, m_send, m_recv, mz_send, mz_recv, f_send, f_recv, a_send, a_recv, z_send, z_recv,
    rs_send, rs_recv, s_send, s_recv, k_send, k_recv, o_send, o_recv,
):
    fields, rows, width = models_ref.shape
    cells = width // group
    half = cells // 2
    slab = group * rows
    count = layers * slab
    chips = group // 2 * planes
    peers = group * planes
    strip = slab // chips
    chunks = fields * 2
    pair = 2 * slab
    total_cells = width * planes
    dom = lax.axis_index("dom")
    y = lax.axis_index("cell")
    z = dom // group
    g = dom % group
    core = g % 2
    chip = g // 2 * planes + y
    near = z // 2
    far = 1 - near
    inner = jnp.logical_and(z > 0, z < layers - 1)
    is_end = jnp.logical_not(inner)
    mate = layers - 1 - z
    tip = near * (layers - 1)
    far_tip = far * (layers - 1)
    toward = jnp.where(inner, mate, 1 + near)
    even = core == 0
    odd = core == 1

    def both(left, right):
        return jnp.logical_and(left, right)

    def at(layer, which):
        return (layer * group + which, y)

    def at_chip(layer, which, kind):
        return (layer * group + which // planes * 2 + kind, which % planes)

    def ring(k):
        return (g, g + 1 - 2 * core, (g + 2) % group, group - 1 - g)[k]

    back = ring

    def remote(src, dst, send, recv, device):
        return pltpu.make_async_remote_copy(
            src_ref=src, dst_ref=dst, send_sem=send, recv_sem=recv,
            device_id=device, device_id_type=MESH,
        )

    loads = [
        pltpu.make_async_copy(models_ref, m_loc, loc_sem.at[0]),
        pltpu.make_async_copy(grads_ref, g_loc, loc_sem.at[1]),
    ]
    for copy in loads:
        copy.start()

    barrier = pltpu.get_barrier_semaphore()
    here = g * planes + y

    def greet(k, carry):
        to = (here + k) % peers
        pl.semaphore_signal(
            barrier, inc=1, device_id=(z * group + to // planes, to % planes), device_id_type=MESH
        )
        return carry

    lax.fori_loop(1, peers, greet, 0)
    pl.semaphore_signal(barrier, inc=1, device_id=at(toward, g), device_id_type=MESH)

    @pl.when(inner)
    def _():
        pl.semaphore_signal(barrier, inc=1, device_id=at(tip, g), device_id_type=MESH)

    @pl.when(z == 1)
    def _():
        pl.semaphore_signal(barrier, inc=1, device_id=at(far_tip, g), device_id_type=MESH)

    pl.semaphore_wait(barrier, peers + jnp.where(z > 0, 1, 0))

    @pl.when(z == 1)
    def _():
        pl.semaphore_signal(ready, inc=1, device_id=at(tip, g), device_id_type=MESH)
        pl.semaphore_signal(ready, inc=1, device_id=at(mate, g), device_id_type=MESH)

    @pl.when(z == 0)
    def _():
        pl.semaphore_signal(ready, inc=1, device_id=at(1, g), device_id_type=MESH)

    def m_part(side, to):
        return models_ref.at[:, :, pl.ds(pl.multiple_of(to * cells + side * half, 128), half)]

    sides = (jnp.where(z == 0, near, far), jnp.where(z == 0, far, near))

    def landing(slot, kind, source):
        return mbuf.at[kind, z, source] if slot else mst.at[source]

    def m_copy(slot, k):
        to = ring(k)
        return remote(
            m_part(sides[slot], to), landing(slot, to % 2, g),
            m_send.at[slot, k], m_recv.at[slot, g], at(z, to),
        )

    def m_own(slot):
        return pltpu.make_async_copy(
            m_part(sides[slot], g), landing(slot, core, g), loc_sem.at[2 + slot]
        )

    def m_hop(slot, k):
        source = back(k)
        src = m_part(sides[slot], g) if k == 0 else landing(slot, core, source)
        return remote(
            src, mbuf.at[core, z, source], mz_send.at[slot, k], mz_recv.at[z, source],
            at(1 + sides[slot], g),
        )

    def m_ready(slot, k):
        source = back(k)
        remote(
            m_part(sides[slot], g), landing(slot, core, source),
            m_send.at[slot, k], m_recv.at[slot, source], at(z, source),
        ).wait_recv()

    for slot in range(2):
        for k in range(1, group):
            m_copy(slot, k).start()
        m_own(slot).start()

    @pl.when(z == layers - 1)
    def _():
        m_hop(1, 0).start()

    m_hop(0, 0).start()

    for copy in loads:
        copy.wait()

    scale = scale_ref[0]

    def a_copy(s, k):
        to = ring(k)
        return remote(
            code.at[s, to], hbuf.at[s, z, g], a_send.at[s, k], a_recv.at[s, g], at(z, to)
        )

    weight = 2.0 * LIFT / jnp.full((rows, half), scale, jnp.float32)
    for s in range(chunks):
        field, side = s // 2, s % 2
        for to in range(group):
            span = slice(to * cells + side * half, to * cells + side * half + half)
            value = g_loc[field, :, span].astype(jnp.float32) * LIFT
            value = value - weight * m_loc[field, :, span].astype(jnp.float32)
            square = value * value
            code[s, to] = (square * square * square * value * jnp.abs(value)).astype(jnp.bfloat16)
        for k in range(1, group):
            a_copy(s, k).start()
        hbuf[s, z, g] = code[s, g]

    def z_copy(s, layer, outward):
        block = hbuf.at[s, layer]
        return remote(
            block, block, z_send.at[outward, s, layer], z_recv.at[s, layer],
            at(tip if outward else toward, g),
        )

    def decode(s, layer):
        value = hbuf[s, layer].reshape(slab, half).astype(jnp.float32)
        root = jnp.exp2(jnp.log2(jnp.abs(value)) * 0.125)
        root = jnp.where(value < 0.0, -root, root)
        upper = root.astype(jnp.bfloat16)
        high[s, layer] = upper
        low[s, layer] = (root - upper.astype(jnp.float32)).astype(jnp.bfloat16)

    def own_ready(s, first=1, last=group):
        for k in range(first, last):
            source = back(k)
            remote(
                code.at[s, g], hbuf.at[s, z, source], a_send.at[s, k], a_recv.at[s, source],
                at(z, source),
            ).wait_recv()

    def z_half(s, side):
        start = (g // 2 + side) % 2 * 2
        block = hbuf.at[s, z, pl.ds(start, 2)]
        return remote(block, block, h_send.at[side, s], z_recv.at[s, z], at(tip, g))

    def z_direct(s, k):
        to = ring(k)
        return remote(
            code.at[s, to], hbuf.at[s, z, g], d_send.at[s, k], z_recv.at[s, z],
            at(jnp.where(z == 1, tip, mate), to),
        )

    def pass_on(s, layer, outward):
        z_copy(s, layer, outward).wait_recv()
        z_copy(s, layer, outward).start()

    def f_copy(kind, layer):
        block = mbuf.at[kind, layer]
        return remote(
            block, block, f_send.at[layer], f_recv.at[layer], at(z, g + 1 - 2 * core)
        )

    def m_wait(layer):
        for k in range(group):
            source = back(k)
            remote(
                m_part(near, g), mbuf.at[core, layer, source], mz_send.at[0, k],
                mz_recv.at[layer, source], at(layer, g),
            ).wait_recv()
        f_copy(core, layer).start()

    contract = (((1,), (1,)), ((), ()))

    def inner_product(left, right):
        return lax.dot_general(left, right, contract, preferred_element_type=jnp.float32)

    def particles(kind, first, size, field):
        return mbuf[kind, first:first + size, :, field].reshape(size * slab, half)

    def gram(left, right):
        total = jnp.zeros((left[1] * slab, right[1] * slab), jnp.float32)
        for kind in range(2):
            for field in range(fields):
                total += inner_product(
                    particles(kind, *left, field), particles(kind, *right, field)
                )
        return total

    def squares(first, size):
        total = jnp.zeros((size * slab, half), jnp.float32)
        for kind in range(2):
            for field in range(fields):
                wide = particles(kind, first, size, field).astype(jnp.float32)
                total += wide * wide
        ones = jnp.ones((8, half), jnp.bfloat16)
        upper = total.astype(jnp.bfloat16)
        rest = total - upper.astype(jnp.float32)
        middle = rest.astype(jnp.bfloat16)
        lower = (rest - middle.astype(jnp.float32)).astype(jnp.bfloat16)
        return (
            inner_product(ones, upper) + inner_product(ones, middle) + inner_product(ones, lower)
        )

    def rs_span(deep):
        return pl.ds(0, 8 + (2 if deep else 1) * strip)

    steps = [(dx, dy) for dx in range(group // 2) for dy in range(planes) if dx + dy]
    steps.sort(key=lambda step: -(step[0] > 0) - (step[1] > 0))

    def chip_at(k, sign):
        dx, dy = steps[k - 1]
        columns = group // 2
        return (g // 2 + columns + sign * dx) % columns * planes + (y + planes + sign * dy) % planes

    def rs_copy(slot, k, deep):
        to = chip_at(k, 1)
        span = rs_span(deep)
        return remote(
            part.at[slot, to, span], inbox.at[slot, chip, span], rs_send.at[slot, k],
            rs_recv.at[slot, chip], at_chip(z, to, core),
        )

    def share(slot, total, norms, deep):
        for q in range(chips):
            first = total[q * strip:(q + 1) * strip]
            second = total[slab + q * strip:slab + (q + 1) * strip]
            part[slot, q, :8] = norms
            if deep:
                part[slot, q, 8:8 + strip] = first
                part[slot, q, 8 + strip:] = second
            else:
                part[slot, q, 8:8 + strip] = jnp.concatenate((first, second), axis=1)
        for k in range(1, chips):
            rs_copy(slot, k, deep).start()

    def collect(slot, deep):
        span = slice(0, 8 + (2 if deep else 1) * strip)
        total = part[slot, chip, span]
        for k in range(1, chips):
            source = chip_at(k, -1)
            remote(
                part.at[slot, chip, rs_span(deep)], inbox.at[slot, source, rs_span(deep)],
                rs_send.at[slot, k], rs_recv.at[slot, source], at_chip(z, source, core),
            ).wait_recv()
            total = total + inbox[slot, source, span]
        return total

    def swap(layer, source):
        return remote(
            swap_out.at[layer], swap_in.at[source], s_send.at[layer], s_recv.at[source],
            at(layer, g),
        )

    def swap_go(layer):
        if layer in (0, layers - 1):
            swap(layer, near).start()
        else:
            pl.when(z != layer)(lambda: swap(layer, near).start())

    def swap_rows(layer, total, row):
        swap_out[layer, :8] = total[:8]
        swap_out[layer, 8:] = total[8 + row * strip:8 + (row + 1) * strip]
        swap_go(layer)

    moves = [
        (dx, dy, dc)
        for dx in range(group // 2) for dy in range(planes) for dc in range(2) if dx + dy + dc
    ]
    moves.sort(key=lambda move: (-(move[0] > 0) - (move[1] > 0), -move[0], move[2]))

    def k_copy(k):
        dx, dy, dc = moves[k]
        to = (g // 2 + dx) % (group // 2) * 2 + (core + dc) % 2
        return remote(
            krow, kin.at[core, chip], k_send.at[k], k_recv.at[core, chip],
            (z * group + to, (y + dy) % planes),
        )

    def k_spread(verb):
        for k in range(peers - 1):
            getattr(k_copy(k), verb)()

    def k_rows(total):
        lanes = lax.broadcasted_iota(jnp.int32, (strip, pair), 1)
        local = lax.broadcasted_iota(jnp.int32, (strip, pair), 0) + chip * strip
        norms = total[0:1]
        first = jnp.sum(jnp.where(lanes == local, norms, 0.0), axis=1, keepdims=True)
        second = jnp.sum(jnp.where(lanes == local + slab, norms, 0.0), axis=1, keepdims=True)
        tall = both(odd, near == 1)
        left = lanes < slab
        upper = z % 2 == 1
        pick = jnp.where(tall, left.astype(jnp.int32), jnp.where(upper, 0, 1))
        own = jnp.where(pick == 1, first, second)
        others = total[4:5]
        distance = own + others - 2.0 * total[8:]
        divisor = jnp.full(distance.shape, scale * total_cells, jnp.float32)
        krow[...] = jnp.exp(-distance / divisor).astype(jnp.bfloat16)
        k_spread("start")
        kin[core, chip] = krow[...]

    @pl.when(z == 0)
    def _():
        pl.semaphore_wait(ready, 1)
        m_hop(1, 0).start()

    m_ready(0, 1)
    m_hop(0, 1).start()

    @pl.when(is_end)
    def _():
        m_ready(1, 1)
        m_hop(1, 1).start()

    @pl.when(inner)
    def _():
        @pl.when(z == 1)
        def _():
            pl.semaphore_wait(ready, 1)
            for s in range(chunks):
                for k in (0, 1, 2, 3):
                    z_direct(s, k).start()

        @pl.when(z != 1)
        def _():
            for s in range(chunks):
                own_ready(s, 1, 2)
                z_half(s, 0).start()

    for k in range(2, group):
        m_ready(0, k)
        m_hop(0, k).start()

    @pl.when(z == 2)
    def _():
        pl.semaphore_wait(ready, 1)
        for s in range(chunks):
            for k in range(group):
                z_direct(s, k).start()

    @pl.when(is_end)
    def _():
        for k in range(2, group):
            m_ready(1, k)
            m_hop(1, k).start()

    @pl.when(inner)
    def _():
        for k in range(1, group):
            m_ready(1, k)
        m_own(1).wait()
        f_copy(core, z).start()
        for s in range(chunks):
            pl.when(z == 1)(lambda: own_ready(s, 1, 2))
            own_ready(s, 2)

            @pl.when(z != 1)
            def _():
                z_half(s, 1).start()
        pl.when(z != 2)(z_copy(0, z, 0).start)
        pl.when(z != 2)(z_copy(1, z, 0).start)
        pl.when(z != 2)(z_copy(2, z, 0).start)
        pl.when(z != 2)(z_copy(3, z, 0).start)
        m_wait(mate)
        m_wait(0)
        for layer in range(layers - 1):
            f_copy(1 - core, layer).wait_recv()

        @pl.when(even)
        def _():
            share(0, gram((0, 2), (0, 2)), squares(0, 2), True)

        @pl.when(odd)
        def _():
            norms = jnp.concatenate(
                (squares(0, 2)[:4], jnp.concatenate((squares(2, 1)[:4],) * 2, axis=1)), axis=0
            )
            share(0, gram((0, 2), (2, 1)), norms, False)

        pass_on(0, mate, 1)
        m_wait(layers - 1)
        f_copy(1 - core, layers - 1).wait_recv()

        @pl.when(even)
        def _():
            share(1, gram((2, 2), (2, 2)), squares(2, 2), True)

        @pl.when(odd)
        def _():
            norms = jnp.concatenate(
                (part[0, 0, :4], jnp.concatenate((squares(3, 1)[:4],) * 2, axis=1)), axis=0
            )
            share(1, gram((0, 2), (3, 1)), norms, False)

        @pl.when(z == 1)
        def _():
            pass_on(1, mate, 1)
            pass_on(2, mate, 1)
            pass_on(3, mate, 1)
            pass_on(0, tip, 0)
            pass_on(1, tip, 0)

        @pl.when(z == 2)
        def _():
            pass_on(0, tip, 0)
            pass_on(1, tip, 0)
            pass_on(1, mate, 1)
            pass_on(2, mate, 1)
            pass_on(3, mate, 1)

        @pl.when(even)
        def _():
            total = collect(0, True)
            swap_rows(0, total, 0)
            swap_rows(1, total, 1)

        @pl.when(odd)
        def _():
            swap_out[2] = collect(0, False)
            swap_go(2)

        decode(0, z)
        decode(1, z)
        decode(2, z)
        decode(3, z)

        @pl.when(even)
        def _():
            total = collect(1, True)
            swap_rows(3, total, 1)
            swap_rows(2, total, 0)

        @pl.when(odd)
        def _():
            third = swap_out[2]
            fourth = collect(1, False)
            for layer in range(2):
                span = slice(layer * slab, (layer + 1) * slab)
                swap_out[layer, :4] = third[:4]
                swap_out[layer, 4:8] = jnp.concatenate(
                    (third[4:8, :slab], fourth[4:8, :slab]), axis=1
                )
                swap_out[layer, 8:] = jnp.concatenate((third[8:, span], fourth[8:, span]), axis=1)
                swap_go(layer)
            swap_out[3] = fourth
            swap_go(3)

        @pl.when(z == 1)
        def _():
            pass_on(0, far_tip, 1)
            pass_on(1, far_tip, 1)
            pass_on(2, tip, 0)
            pass_on(3, tip, 0)

        @pl.when(z == 2)
        def _():
            pass_on(2, tip, 0)
            pass_on(3, tip, 0)
            pass_on(0, far_tip, 1)
            pass_on(1, far_tip, 1)

        decode(0, tip)
        decode(1, tip)
        decode(2, tip)
        decode(3, tip)
        swap(mate, far).wait_recv()
        k_rows(swap_out[z] + swap_in[far])
        pass_on(2, far_tip, 1)
        pass_on(3, far_tip, 1)
        decode(0, mate)
        decode(1, mate)
        decode(2, mate)
        decode(3, mate)
        decode(0, far_tip)
        decode(1, far_tip)
        decode(2, far_tip)
        decode(3, far_tip)

    @pl.when(is_end)
    def _():
        m_own(1).wait()
        for s in range(chunks):
            own_ready(s)
            z_copy(s, z, 0).start()
        for s in range(chunks):
            decode(s, z)
        for s in range(chunks):
            z_copy(s, toward, 0).wait_recv()
            decode(s, toward)
        swap(toward, near).wait_recv()
        swap(mate, far).wait_recv()
        k_rows(swap_in[0] + swap_in[1])
        for s in range(chunks):
            z_copy(s, layers - 1 - toward, 0).wait_recv()
            decode(s, layers - 1 - toward)
        for s in range(1):
            z_copy(s, mate, 0).wait_recv()
            decode(s, mate)

    def k_ready(kind, k):
        q = (chip + k) % chips
        remote(
            krow, kin.at[kind, q], k_send.at[0], k_recv.at[kind, q], at(z, back(1))
        ).wait_recv()

    k_ready(1 - core, 0)
    for k in range(1, chips):
        k_ready(0, k)
        k_ready(1, k)

    @pl.when(near == 0)
    def _():
        kfull[:, :pair] = kin[0].reshape(slab, pair)
        kfull[:, pair:] = kin[1].reshape(slab, pair)

    @pl.when(near == 1)
    def _():
        kfull[:, pair:] = kin[0].reshape(slab, pair)
        tall = kin[1].reshape(slab, pair).astype(jnp.float32)
        kfull[:, :slab] = tall[:, :slab].T.astype(jnp.bfloat16)
        kfull[:, slab:pair] = tall[:, slab:].T.astype(jnp.bfloat16)

    rowsum = jnp.sum(kfull[...].astype(jnp.float32), axis=1, keepdims=True)
    pull = 2.0 / jnp.full((slab, 1), scale, jnp.float32) * rowsum
    m_own(0).wait()

    def o_own(s):
        span = pl.ds(pl.multiple_of(g * cells + s % 2 * half, 128), half)
        return pltpu.make_async_copy(
            outbox.at[s, g], out_ref.at[s // 2, :, span], own_sem.at[s]
        )

    def o_copy(s, k):
        field, side = s // 2, s % 2
        to = ring(k)
        span = pl.ds(pl.multiple_of(g * cells + side * half, 128), half)
        return remote(
            outbox.at[s, to], out_ref.at[field, :, span], o_send.at[s, k], o_recv.at[s, g],
            at(z, to),
        )

    for s in range(chunks):
        field, side = s // 2, s % 2

        if s >= 1:
            @pl.when(is_end)
            def _():
                z_copy(s, mate, 0).wait_recv()
                decode(s, mate)

        kernel = kfull[...]
        update = jnp.dot(
            kernel, high[s].reshape(count, half), preferred_element_type=jnp.float32
        ) + jnp.dot(kernel, low[s].reshape(count, half), preferred_element_type=jnp.float32)
        own = jnp.where(sides[1] == side, mbuf[core, z, :, field], mst[:, field])
        own = own.reshape(slab, half).astype(jnp.float32)
        update = update * (1.0 / LIFT) + pull * own
        square = update * update
        update = square * square * square * update * jnp.abs(update)
        outbox[s] = update.astype(jnp.bfloat16).reshape(group, rows, half)
        for k in (2, 3, 1):
            o_copy(s, k).start()
        o_own(s).start()

    for k in range(1, group):
        m_copy(0, k).wait_send()
        m_copy(1, k).wait_send()
    for k in range(group):
        m_hop(0, k).wait_send()

    @pl.when(is_end)
    def _():
        for k in range(group):
            m_hop(1, k).wait_send()
    for s in range(chunks):
        for k in range(1, group):
            a_copy(s, k).wait_send()
        pl.when(z != 2)(z_copy(s, z, 0).wait_send)

    @pl.when(inner)
    def _():
        for layer in range(layers):
            f_copy(core, layer).wait_send()
        for s in range(chunks):
            for k in range(group):
                z_direct(s, k).wait_send()

            @pl.when(z != 1)
            def _():
                z_half(s, 0).wait_send()
                z_half(s, 1).wait_send()

            z_copy(s, tip, 0).wait_send()
            z_copy(s, mate, 1).wait_send()
            z_copy(s, far_tip, 1).wait_send()
        for slot in range(2):
            for k in range(1, chips):
                @pl.when(even)
                def _():
                    rs_copy(slot, k, True).wait_send()

                @pl.when(odd)
                def _():
                    rs_copy(slot, k, False).wait_send()

        swap(0, near).wait_send()
        swap(layers - 1, near).wait_send()
        swap(mate, near).wait_send()

    k_spread("wait_send")

    for s in range(chunks):
        field, side = s // 2, s % 2
        o_own(s).wait()
        for k in range(1, group):
            o_copy(s, k).wait_send()
            source = back(k)
            span = pl.ds(pl.multiple_of(source * cells + side * half, 128), half)
            remote(
                outbox.at[s, source], out_ref.at[field, :, span], o_send.at[s, k],
                o_recv.at[s, source], at(z, source),
            ).wait_recv()


def expand_kernel(factor, code_ref, out_ref):
    wide = code_ref[...].astype(jnp.float32)
    root = jnp.exp2(jnp.log2(jnp.abs(wide)) * 0.125) * factor
    out_ref[...] = jnp.where(wide < 0.0, -root, root)


def fused_body(layers, group, planes, models, gradients, length_scale):
    fields, rows, width = models.shape
    cells = width // group
    half = cells // 2
    slab = group * rows
    count = layers * slab
    chips = group // 2 * planes
    strip = slab // chips
    chunks = fields * 2
    pair = 2 * slab
    peers = group * planes
    dma = pltpu.SemaphoreType.DMA
    vmem = pltpu.VMEM
    gathered = pl.pallas_call(
        functools.partial(stein_kernel, layers, group, planes),
        out_shape=jax.ShapeDtypeStruct(models.shape, jnp.bfloat16),
        in_specs=[
            pl.BlockSpec(memory_space=pltpu.SMEM),
            pl.BlockSpec(memory_space=pl.ANY),
            pl.BlockSpec(memory_space=pl.ANY),
        ],
        out_specs=pl.BlockSpec(memory_space=pl.ANY),
        scratch_shapes=[
            vmem(models.shape, jnp.bfloat16),
            vmem(models.shape, jnp.bfloat16),
            vmem((chunks, group, rows, half), jnp.bfloat16),
            vmem((group, fields, rows, half), jnp.bfloat16),
            vmem((2, layers, group, fields, rows, half), jnp.bfloat16),
            vmem((chunks, layers, group, rows, half), jnp.bfloat16),
            vmem((chunks, layers, slab, half), jnp.bfloat16),
            vmem((chunks, layers, slab, half), jnp.bfloat16),
            vmem((2, chips, 8 + 2 * strip, pair), jnp.float32),
            vmem((2, chips, 8 + 2 * strip, pair), jnp.float32),
            vmem((layers, 8 + strip, pair), jnp.float32),
            vmem((2, 8 + strip, pair), jnp.float32),
            vmem((strip, pair), jnp.bfloat16),
            vmem((2, chips, strip, pair), jnp.bfloat16),
            vmem((slab, count), jnp.bfloat16),
            vmem((chunks, group, rows, half), jnp.bfloat16),
            pltpu.SemaphoreType.REGULAR,
            dma((chunks, group)),
            dma((chunks,)),
            dma((2, chunks)),
            dma((4,)),
            dma((2, group)),
            dma((2, group)),
            dma((2, group)),
            dma((layers, group)),
            dma((layers,)),
            dma((layers,)),
            dma((chunks, group)),
            dma((chunks, group)),
            dma((2, chunks, layers)),
            dma((chunks, layers)),
            dma((2, chips)),
            dma((2, chips)),
            dma((layers,)),
            dma((2,)),
            dma((peers,)),
            dma((2, chips)),
            dma((chunks, group)),
            dma((chunks, group)),
        ],
        compiler_params=pltpu.CompilerParams(collective_id=0, has_side_effects=True),
        name="stein",
    )(length_scale, models, gradients)
    return pl.pallas_call(
        functools.partial(expand_kernel, 1.0 / count),
        out_shape=jax.ShapeDtypeStruct(models.shape, jnp.float32),
        grid=(fields,),
        in_specs=[pl.BlockSpec((1, rows, width), lambda i: (i, 0, 0))],
        out_specs=pl.BlockSpec((1, rows, width), lambda i: (i, 0, 0)),
        name="expand",
    )(gathered)


def solution(mesh):
    spread, planes = mesh.shape["dom"], mesh.shape["cell"]
    layers = math.isqrt(spread)
    group = spread // layers

    def body(models, gradients, length_scale):
        _, rows, width = models.shape
        slab = group * rows
        chips = group // 2 * planes
        fits = (
            layers == 4
            and group == 4
            and models.shape[0] == 2
            and layers * group == spread
            and width % (group * 256) == 0
            and rows % 16 == 0
            and slab % 128 == 0
            and slab % (chips * 16) == 0
        )
        if not fits:
            return plain_body(models, gradients, length_scale)
        return fused_body(layers, group, planes, models, gradients, length_scale)

    placed = (P(None, "dom", "cell"), P(None, "dom", "cell"), P())
    return jax.shard_map(
        body, mesh=mesh, in_specs=placed, out_specs=P(None, "dom", "cell"), check_vma=False
    )
```

```python
import functools
import math

import jax
import jax.numpy as jnp
from jax import lax
from jax.experimental import pallas as pl
from jax.experimental.pallas import tpu as pltpu
from jax.sharding import PartitionSpec as P

MESH = pl.DeviceIdType.MESH


def plain_body(models, gradients, length_scale):
    local_models, local_grads = (
        lax.all_to_all(models, "dom", split_axis=2, concat_axis=1, tiled=True),
        lax.all_to_all(gradients, "dom", split_axis=2, concat_axis=1, tiled=True),
    )
    cell_block = local_models.shape[2]
    particles = local_models.shape[1]
    cell_count = cell_block * lax.axis_size("dom") * lax.axis_size("cell")
    scale_value = length_scale[0]
    divisor = scale_value * cell_count
    partial_value = jnp.einsum(
        "kpc,kqc->pq", local_models, local_models, preferred_element_type=jnp.float32
    )
    summed = lax.psum(partial_value, "cell")
    row_block = lax.psum_scatter(summed, "dom", scatter_dimension=0, tiled=True)
    row_count = row_block.shape[0]
    row_start = lax.axis_index("dom") * row_count
    own_squares = jnp.diagonal(lax.dynamic_slice_in_dim(row_block, row_start, row_count, 1))
    squares = lax.all_gather(own_squares, "dom", axis=0, tiled=True)
    distance = own_squares[:, None] + squares[None, :] - 2.0 * row_block
    kernel = lax.all_gather(
        jnp.exp(-distance / divisor).astype(jnp.bfloat16), "dom", axis=0, tiled=True
    )
    rowsum = jnp.sum(kernel.astype(jnp.float32), axis=1)
    stacked = jnp.concatenate((local_grads, local_models), axis=2)
    product = jnp.einsum("pq,kqc->kpc", kernel, stacked, preferred_element_type=jnp.float32)
    attract = product[:, :, :cell_block]
    pulled = product[:, :, cell_block:]
    update = (
        attract
        + 2.0 / scale_value * (rowsum[None, :, None] * local_models.astype(jnp.float32) - pulled)
    ) / particles
    return lax.all_to_all(update, "dom", split_axis=1, concat_axis=2, tiled=True)


LIFT = 512.0


def stein_kernel(
    layers, group, planes,
    scale_ref, models_ref, grads_ref, out_ref,
    m_loc, g_loc, code, mst, mbuf, hbuf, high, low, part, inbox, swap_out, swap_in,
    krow, kin, kfull, outbox,
    ready, d_send, own_sem, h_send, loc_sem, m_send, m_recv, mz_send, mz_recv, f_send, f_recv, a_send, a_recv, z_send, z_recv,
    rs_send, rs_recv, s_send, s_recv, k_send, k_recv, o_send, o_recv,
):
    fields, rows, width = models_ref.shape
    cells = width // group
    half = cells // 2
    slab = group * rows
    count = layers * slab
    chips = group // 2 * planes
    peers = group * planes
    strip = slab // chips
    chunks = fields * 2
    pair = 2 * slab
    total_cells = width * planes
    dom = lax.axis_index("dom")
    y = lax.axis_index("cell")
    z = dom // group
    g = dom % group
    core = g % 2
    chip = g // 2 * planes + y
    near = z // 2
    far = 1 - near
    inner = jnp.logical_and(z > 0, z < layers - 1)
    is_end = jnp.logical_not(inner)
    mate = layers - 1 - z
    tip = near * (layers - 1)
    far_tip = far * (layers - 1)
    toward = jnp.where(inner, mate, 1 + near)
    even = core == 0
    odd = core == 1

    def both(left, right):
        return jnp.logical_and(left, right)

    def at(layer, which):
        return (layer * group + which, y)

    def at_chip(layer, which, kind):
        return (layer * group + which // planes * 2 + kind, which % planes)

    def ring(k):
        return (g, g + 1 - 2 * core, (g + 2) % group, group - 1 - g)[k]

    back = ring

    def remote(src, dst, send, recv, device):
        return pltpu.make_async_remote_copy(
            src_ref=src, dst_ref=dst, send_sem=send, recv_sem=recv,
            device_id=device, device_id_type=MESH,
        )

    loads = [
        pltpu.make_async_copy(models_ref, m_loc, loc_sem.at[0]),
        pltpu.make_async_copy(grads_ref, g_loc, loc_sem.at[1]),
    ]
    for copy in loads:
        copy.start()

    barrier = pltpu.get_barrier_semaphore()
    here = g * planes + y

    def greet(k, carry):
        to = (here + k) % peers
        pl.semaphore_signal(
            barrier, inc=1, device_id=(z * group + to // planes, to % planes), device_id_type=MESH
        )
        return carry

    lax.fori_loop(1, peers, greet, 0)
    pl.semaphore_signal(barrier, inc=1, device_id=at(toward, g), device_id_type=MESH)

    @pl.when(inner)
    def _():
        pl.semaphore_signal(barrier, inc=1, device_id=at(tip, g), device_id_type=MESH)

    @pl.when(z == 1)
    def _():
        pl.semaphore_signal(barrier, inc=1, device_id=at(far_tip, g), device_id_type=MESH)

    pl.semaphore_wait(barrier, peers + jnp.where(z > 0, 1, 0))

    @pl.when(z == 1)
    def _():
        pl.semaphore_signal(ready, inc=1, device_id=at(tip, g), device_id_type=MESH)
        pl.semaphore_signal(ready, inc=1, device_id=at(mate, g), device_id_type=MESH)

    @pl.when(z == 0)
    def _():
        pl.semaphore_signal(ready, inc=1, device_id=at(1, g), device_id_type=MESH)

    def m_part(side, to):
        return m_loc.at[:, :, pl.ds(pl.multiple_of(to * cells + side * half, 128), half)]

    sides = (jnp.where(z == 0, near, far), jnp.where(z == 0, far, near))

    def landing(slot, kind, source):
        return mbuf.at[kind, z, source] if slot else mst.at[source]

    def m_copy(slot, k):
        to = ring(k)
        return remote(
            m_part(sides[slot], to), landing(slot, to % 2, g),
            m_send.at[slot, k], m_recv.at[slot, g], at(z, to),
        )

    def m_own(slot):
        return pltpu.make_async_copy(
            m_part(sides[slot], g), landing(slot, core, g), loc_sem.at[2 + slot]
        )

    def m_hop(slot, k):
        source = back(k)
        src = m_part(sides[slot], g) if k == 0 else landing(slot, core, source)
        return remote(
            src, mbuf.at[core, z, source], mz_send.at[slot, k], mz_recv.at[z, source],
            at(1 + sides[slot], g),
        )

    def m_ready(slot, k):
        source = back(k)
        remote(
            m_part(sides[slot], g), landing(slot, core, source),
            m_send.at[slot, k], m_recv.at[slot, source], at(z, source),
        ).wait_recv()

    loads[0].wait()
    for slot in range(2):
        for k in range(1, group):
            m_copy(slot, k).start()
        m_own(slot).start()

    @pl.when(z == layers - 1)
    def _():
        m_hop(1, 0).start()

    m_hop(0, 0).start()

    loads[1].wait()

    scale = scale_ref[0]

    def a_copy(s, k):
        to = ring(k)
        return remote(
            code.at[s, to], hbuf.at[s, z, g], a_send.at[s, k], a_recv.at[s, g], at(z, to)
        )

    weight = 2.0 * LIFT / jnp.full((rows, half), scale, jnp.float32)
    for s in range(chunks):
        field, side = s // 2, s % 2
        for to in range(group):
            span = slice(to * cells + side * half, to * cells + side * half + half)
            value = g_loc[field, :, span].astype(jnp.float32) * LIFT
            value = value - weight * m_loc[field, :, span].astype(jnp.float32)
            square = value * value
            code[s, to] = (square * square * square * value * jnp.abs(value)).astype(jnp.bfloat16)
        for k in (2, 3, 1):
            a_copy(s, k).start()
        hbuf[s, z, g] = code[s, g]

    def z_copy(s, layer, outward):
        block = hbuf.at[s, layer]
        return remote(
            block, block, z_send.at[outward, s, layer], z_recv.at[s, layer],
            at(tip if outward else toward, g),
        )

    def decode(s, layer):
        value = hbuf[s, layer].reshape(slab, half).astype(jnp.float32)
        root = jnp.exp2(jnp.log2(jnp.abs(value)) * 0.125)
        root = jnp.where(value < 0.0, -root, root)
        upper = root.astype(jnp.bfloat16)
        high[s, layer] = upper
        low[s, layer] = (root - upper.astype(jnp.float32)).astype(jnp.bfloat16)

    def own_ready(s, first=1, last=group):
        for k in range(first, last):
            source = back(k)
            remote(
                code.at[s, g], hbuf.at[s, z, source], a_send.at[s, k], a_recv.at[s, source],
                at(z, source),
            ).wait_recv()

    def z_half(s, side):
        start = (g // 2 + side) % 2 * 2
        block = hbuf.at[s, z, pl.ds(start, 2)]
        return remote(block, block, h_send.at[side, s], z_recv.at[s, z], at(tip, g))

    def z_direct(s, k):
        to = ring(k)
        return remote(
            code.at[s, to], hbuf.at[s, z, g], d_send.at[s, k], z_recv.at[s, z],
            at(jnp.where(z == 1, tip, mate), to),
        )

    def pass_on(s, layer, outward):
        z_copy(s, layer, outward).wait_recv()
        z_copy(s, layer, outward).start()

    def f_copy(kind, layer):
        block = mbuf.at[kind, layer]
        return remote(
            block, block, f_send.at[layer], f_recv.at[layer], at(z, g + 1 - 2 * core)
        )

    def m_wait(layer):
        for k in range(group):
            source = back(k)
            remote(
                m_part(near, g), mbuf.at[core, layer, source], mz_send.at[0, k],
                mz_recv.at[layer, source], at(layer, g),
            ).wait_recv()
        f_copy(core, layer).start()

    contract = (((1,), (1,)), ((), ()))

    def inner_product(left, right):
        return lax.dot_general(left, right, contract, preferred_element_type=jnp.float32)

    def particles(kind, first, size, field):
        return mbuf[kind, first:first + size, :, field].reshape(size * slab, half)

    def gram(left, right):
        total = jnp.zeros((left[1] * slab, right[1] * slab), jnp.float32)
        for kind in range(2):
            for field in range(fields):
                total += inner_product(
                    particles(kind, *left, field), particles(kind, *right, field)
                )
        return total

    def squares(first, size):
        total = jnp.zeros((size * slab, half), jnp.float32)
        for kind in range(2):
            for field in range(fields):
                wide = particles(kind, first, size, field).astype(jnp.float32)
                total += wide * wide
        ones = jnp.ones((8, half), jnp.bfloat16)
        upper = total.astype(jnp.bfloat16)
        rest = total - upper.astype(jnp.float32)
        middle = rest.astype(jnp.bfloat16)
        lower = (rest - middle.astype(jnp.float32)).astype(jnp.bfloat16)
        return (
            inner_product(ones, upper) + inner_product(ones, middle) + inner_product(ones, lower)
        )

    def rs_span(deep):
        return pl.ds(0, 8 + (2 if deep else 1) * strip)

    steps = [(dx, dy) for dx in range(group // 2) for dy in range(planes) if dx + dy]
    steps.sort(key=lambda step: -(step[0] > 0) - (step[1] > 0))

    def chip_at(k, sign):
        dx, dy = steps[k - 1]
        columns = group // 2
        return (g // 2 + columns + sign * dx) % columns * planes + (y + planes + sign * dy) % planes

    def rs_copy(slot, k, deep):
        to = chip_at(k, 1)
        span = rs_span(deep)
        return remote(
            part.at[slot, to, span], inbox.at[slot, chip, span], rs_send.at[slot, k],
            rs_recv.at[slot, chip], at_chip(z, to, core),
        )

    def share(slot, total, norms, deep):
        for q in range(chips):
            first = total[q * strip:(q + 1) * strip]
            second = total[slab + q * strip:slab + (q + 1) * strip]
            part[slot, q, :8] = norms
            if deep:
                part[slot, q, 8:8 + strip] = first
                part[slot, q, 8 + strip:] = second
            else:
                part[slot, q, 8:8 + strip] = jnp.concatenate((first, second), axis=1)
        for k in range(1, chips):
            rs_copy(slot, k, deep).start()

    def collect(slot, deep):
        span = slice(0, 8 + (2 if deep else 1) * strip)
        total = part[slot, chip, span]
        for k in range(1, chips):
            source = chip_at(k, -1)
            remote(
                part.at[slot, chip, rs_span(deep)], inbox.at[slot, source, rs_span(deep)],
                rs_send.at[slot, k], rs_recv.at[slot, source], at_chip(z, source, core),
            ).wait_recv()
            total = total + inbox[slot, source, span]
        return total

    def swap(layer, source):
        return remote(
            swap_out.at[layer], swap_in.at[source], s_send.at[layer], s_recv.at[source],
            at(layer, g),
        )

    def swap_go(layer):
        if layer in (0, layers - 1):
            swap(layer, near).start()
        else:
            pl.when(z != layer)(lambda: swap(layer, near).start())

    def swap_rows(layer, total, row):
        swap_out[layer, :8] = total[:8]
        swap_out[layer, 8:] = total[8 + row * strip:8 + (row + 1) * strip]
        swap_go(layer)

    moves = [
        (dx, dy, dc)
        for dx in range(group // 2) for dy in range(planes) for dc in range(2) if dx + dy + dc
    ]
    moves.sort(key=lambda move: (-(move[0] > 0) - (move[1] > 0), -move[0], move[2]))

    def k_copy(k):
        dx, dy, dc = moves[k]
        to = (g // 2 + dx) % (group // 2) * 2 + (core + dc) % 2
        return remote(
            krow, kin.at[core, chip], k_send.at[k], k_recv.at[core, chip],
            (z * group + to, (y + dy) % planes),
        )

    def k_spread(verb):
        for k in range(peers - 1):
            getattr(k_copy(k), verb)()

    def k_rows(total):
        lanes = lax.broadcasted_iota(jnp.int32, (strip, pair), 1)
        local = lax.broadcasted_iota(jnp.int32, (strip, pair), 0) + chip * strip
        norms = total[0:1]
        first = jnp.sum(jnp.where(lanes == local, norms, 0.0), axis=1, keepdims=True)
        second = jnp.sum(jnp.where(lanes == local + slab, norms, 0.0), axis=1, keepdims=True)
        tall = both(odd, near == 1)
        left = lanes < slab
        upper = z % 2 == 1
        pick = jnp.where(tall, left.astype(jnp.int32), jnp.where(upper, 0, 1))
        own = jnp.where(pick == 1, first, second)
        others = total[4:5]
        distance = own + others - 2.0 * total[8:]
        divisor = jnp.full(distance.shape, scale * total_cells, jnp.float32)
        krow[...] = jnp.exp(-distance / divisor).astype(jnp.bfloat16)
        k_spread("start")
        kin[core, chip] = krow[...]

    @pl.when(z == 0)
    def _():
        pl.semaphore_wait(ready, 1)
        m_hop(1, 0).start()

    m_ready(0, 1)
    m_hop(0, 1).start()

    @pl.when(is_end)
    def _():
        m_ready(1, 1)
        m_hop(1, 1).start()

    @pl.when(inner)
    def _():
        @pl.when(z == 1)
        def _():
            pl.semaphore_wait(ready, 1)
            for s in range(chunks):
                for k in (0, 1, 2, 3):
                    z_direct(s, k).start()

        @pl.when(z != 1)
        def _():
            for s in range(chunks):
                own_ready(s, 1, 2)
                z_half(s, 0).start()

    for k in range(2, group):
        m_ready(0, k)
        m_hop(0, k).start()

    @pl.when(z == 2)
    def _():
        pl.semaphore_wait(ready, 1)
        for s in range(chunks):
            for k in range(group):
                z_direct(s, k).start()

    @pl.when(is_end)
    def _():
        for k in range(2, group):
            m_ready(1, k)
            m_hop(1, k).start()

    @pl.when(inner)
    def _():
        for k in range(1, group):
            m_ready(1, k)
        m_own(1).wait()
        f_copy(core, z).start()
        for s in range(chunks):
            pl.when(z == 1)(lambda: own_ready(s, 1, 2))
            own_ready(s, 2)

            @pl.when(z != 1)
            def _():
                z_half(s, 1).start()
        pl.when(z != 2)(z_copy(0, z, 0).start)
        pl.when(z != 2)(z_copy(1, z, 0).start)
        pl.when(z != 2)(z_copy(2, z, 0).start)
        pl.when(z != 2)(z_copy(3, z, 0).start)
        m_wait(mate)
        m_wait(0)
        for layer in range(layers - 1):
            f_copy(1 - core, layer).wait_recv()

        @pl.when(even)
        def _():
            share(0, gram((0, 2), (0, 2)), squares(0, 2), True)

        @pl.when(odd)
        def _():
            norms = jnp.concatenate(
                (squares(0, 2)[:4], jnp.concatenate((squares(2, 1)[:4],) * 2, axis=1)), axis=0
            )
            share(0, gram((0, 2), (2, 1)), norms, False)

        pass_on(0, mate, 1)
        m_wait(layers - 1)
        f_copy(1 - core, layers - 1).wait_recv()

        @pl.when(even)
        def _():
            share(1, gram((2, 2), (2, 2)), squares(2, 2), True)

        @pl.when(odd)
        def _():
            norms = jnp.concatenate(
                (part[0, 0, :4], jnp.concatenate((squares(3, 1)[:4],) * 2, axis=1)), axis=0
            )
            share(1, gram((0, 2), (3, 1)), norms, False)

        @pl.when(z == 1)
        def _():
            pass_on(1, mate, 1)
            pass_on(2, mate, 1)
            pass_on(3, mate, 1)
            pass_on(0, tip, 0)
            pass_on(1, tip, 0)

        @pl.when(z == 2)
        def _():
            pass_on(0, tip, 0)
            pass_on(1, tip, 0)
            pass_on(1, mate, 1)
            pass_on(2, mate, 1)
            pass_on(3, mate, 1)

        @pl.when(even)
        def _():
            total = collect(0, True)
            swap_rows(0, total, 0)
            swap_rows(1, total, 1)

        @pl.when(odd)
        def _():
            swap_out[2] = collect(0, False)
            swap_go(2)

        decode(0, z)
        decode(1, z)
        decode(2, z)
        decode(3, z)

        @pl.when(even)
        def _():
            total = collect(1, True)
            swap_rows(3, total, 1)
            swap_rows(2, total, 0)

        @pl.when(odd)
        def _():
            third = swap_out[2]
            fourth = collect(1, False)
            for layer in range(2):
                span = slice(layer * slab, (layer + 1) * slab)
                swap_out[layer, :4] = third[:4]
                swap_out[layer, 4:8] = jnp.concatenate(
                    (third[4:8, :slab], fourth[4:8, :slab]), axis=1
                )
                swap_out[layer, 8:] = jnp.concatenate((third[8:, span], fourth[8:, span]), axis=1)
                swap_go(layer)
            swap_out[3] = fourth
            swap_go(3)

        @pl.when(z == 1)
        def _():
            pass_on(0, far_tip, 1)
            pass_on(1, far_tip, 1)
            pass_on(2, tip, 0)
            pass_on(3, tip, 0)

        @pl.when(z == 2)
        def _():
            pass_on(2, tip, 0)
            pass_on(3, tip, 0)
            pass_on(0, far_tip, 1)
            pass_on(1, far_tip, 1)

        decode(0, tip)
        decode(1, tip)
        decode(2, tip)
        decode(3, tip)
        swap(mate, far).wait_recv()
        k_rows(swap_out[z] + swap_in[far])
        pass_on(2, far_tip, 1)
        pass_on(3, far_tip, 1)
        decode(0, mate)
        decode(1, mate)
        decode(2, mate)
        decode(3, mate)
        decode(0, far_tip)
        decode(1, far_tip)
        decode(2, far_tip)
        decode(3, far_tip)

    @pl.when(is_end)
    def _():
        m_own(1).wait()
        for s in range(chunks):
            own_ready(s)
            z_copy(s, z, 0).start()
        for s in range(chunks):
            decode(s, z)
        for s in range(chunks):
            z_copy(s, toward, 0).wait_recv()
            decode(s, toward)
        swap(toward, near).wait_recv()
        swap(mate, far).wait_recv()
        k_rows(swap_in[0] + swap_in[1])
        for s in range(chunks):
            z_copy(s, layers - 1 - toward, 0).wait_recv()
            decode(s, layers - 1 - toward)
        for s in range(1):
            z_copy(s, mate, 0).wait_recv()
            decode(s, mate)

    def k_ready(kind, k):
        q = (chip + k) % chips
        remote(
            krow, kin.at[kind, q], k_send.at[0], k_recv.at[kind, q], at(z, back(1))
        ).wait_recv()

    k_ready(1 - core, 0)
    for k in range(1, chips):
        k_ready(0, k)
        k_ready(1, k)

    @pl.when(near == 0)
    def _():
        kfull[:, :pair] = kin[0].reshape(slab, pair)
        kfull[:, pair:] = kin[1].reshape(slab, pair)

    @pl.when(near == 1)
    def _():
        kfull[:, pair:] = kin[0].reshape(slab, pair)
        tall = kin[1].reshape(slab, pair).astype(jnp.float32)
        kfull[:, :slab] = tall[:, :slab].T.astype(jnp.bfloat16)
        kfull[:, slab:pair] = tall[:, slab:].T.astype(jnp.bfloat16)

    rowsum = jnp.sum(kfull[...].astype(jnp.float32), axis=1, keepdims=True)
    pull = 2.0 / jnp.full((slab, 1), scale, jnp.float32) * rowsum
    m_own(0).wait()

    def o_own(s):
        span = pl.ds(pl.multiple_of(g * cells + s % 2 * half, 128), half)
        return pltpu.make_async_copy(
            outbox.at[s, g], out_ref.at[s // 2, :, span], own_sem.at[s]
        )

    def o_copy(s, k):
        field, side = s // 2, s % 2
        to = ring(k)
        span = pl.ds(pl.multiple_of(g * cells + side * half, 128), half)
        return remote(
            outbox.at[s, to], out_ref.at[field, :, span], o_send.at[s, k], o_recv.at[s, g],
            at(z, to),
        )

    for s in range(chunks):
        field, side = s // 2, s % 2

        if s >= 1:
            @pl.when(is_end)
            def _():
                z_copy(s, mate, 0).wait_recv()
                decode(s, mate)

        kernel = kfull[...]
        update = jnp.dot(
            kernel, high[s].reshape(count, half), preferred_element_type=jnp.float32
        ) + jnp.dot(kernel, low[s].reshape(count, half), preferred_element_type=jnp.float32)
        own = jnp.where(sides[1] == side, mbuf[core, z, :, field], mst[:, field])
        own = own.reshape(slab, half).astype(jnp.float32)
        update = update * (1.0 / LIFT) + pull * own
        square = update * update
        update = square * square * square * update * jnp.abs(update)
        outbox[s] = update.astype(jnp.bfloat16).reshape(group, rows, half)
        for k in (2, 3, 1):
            o_copy(s, k).start()
        o_own(s).start()

    for k in range(1, group):
        m_copy(0, k).wait_send()
        m_copy(1, k).wait_send()
    for k in range(group):
        m_hop(0, k).wait_send()

    @pl.when(is_end)
    def _():
        for k in range(group):
            m_hop(1, k).wait_send()
    for s in range(chunks):
        for k in range(1, group):
            a_copy(s, k).wait_send()
        pl.when(z != 2)(z_copy(s, z, 0).wait_send)

    @pl.when(inner)
    def _():
        for layer in range(layers):
            f_copy(core, layer).wait_send()
        for s in range(chunks):
            for k in range(group):
                z_direct(s, k).wait_send()

            @pl.when(z != 1)
            def _():
                z_half(s, 0).wait_send()
                z_half(s, 1).wait_send()

            z_copy(s, tip, 0).wait_send()
            z_copy(s, mate, 1).wait_send()
            z_copy(s, far_tip, 1).wait_send()
        for slot in range(2):
            for k in range(1, chips):
                @pl.when(even)
                def _():
                    rs_copy(slot, k, True).wait_send()

                @pl.when(odd)
                def _():
                    rs_copy(slot, k, False).wait_send()

        swap(0, near).wait_send()
        swap(layers - 1, near).wait_send()
        swap(mate, near).wait_send()

    k_spread("wait_send")

    for s in range(chunks):
        field, side = s // 2, s % 2
        o_own(s).wait()
        for k in range(1, group):
            o_copy(s, k).wait_send()
            source = back(k)
            span = pl.ds(pl.multiple_of(source * cells + side * half, 128), half)
            remote(
                outbox.at[s, source], out_ref.at[field, :, span], o_send.at[s, k],
                o_recv.at[s, source], at(z, source),
            ).wait_recv()


def expand_kernel(factor, code_ref, out_ref):
    wide = code_ref[...].astype(jnp.float32)
    root = jnp.exp2(jnp.log2(jnp.abs(wide)) * 0.125) * factor
    out_ref[...] = jnp.where(wide < 0.0, -root, root)


def fused_body(layers, group, planes, models, gradients, length_scale):
    fields, rows, width = models.shape
    cells = width // group
    half = cells // 2
    slab = group * rows
    count = layers * slab
    chips = group // 2 * planes
    strip = slab // chips
    chunks = fields * 2
    pair = 2 * slab
    peers = group * planes
    dma = pltpu.SemaphoreType.DMA
    vmem = pltpu.VMEM
    gathered = pl.pallas_call(
        functools.partial(stein_kernel, layers, group, planes),
        out_shape=jax.ShapeDtypeStruct(models.shape, jnp.bfloat16),
        in_specs=[
            pl.BlockSpec(memory_space=pltpu.SMEM),
            pl.BlockSpec(memory_space=pl.ANY),
            pl.BlockSpec(memory_space=pl.ANY),
        ],
        out_specs=pl.BlockSpec(memory_space=pl.ANY),
        scratch_shapes=[
            vmem(models.shape, jnp.bfloat16),
            vmem(models.shape, jnp.bfloat16),
            vmem((chunks, group, rows, half), jnp.bfloat16),
            vmem((group, fields, rows, half), jnp.bfloat16),
            vmem((2, layers, group, fields, rows, half), jnp.bfloat16),
            vmem((chunks, layers, group, rows, half), jnp.bfloat16),
            vmem((chunks, layers, slab, half), jnp.bfloat16),
            vmem((chunks, layers, slab, half), jnp.bfloat16),
            vmem((2, chips, 8 + 2 * strip, pair), jnp.float32),
            vmem((2, chips, 8 + 2 * strip, pair), jnp.float32),
            vmem((layers, 8 + strip, pair), jnp.float32),
            vmem((2, 8 + strip, pair), jnp.float32),
            vmem((strip, pair), jnp.bfloat16),
            vmem((2, chips, strip, pair), jnp.bfloat16),
            vmem((slab, count), jnp.bfloat16),
            vmem((chunks, group, rows, half), jnp.bfloat16),
            pltpu.SemaphoreType.REGULAR,
            dma((chunks, group)),
            dma((chunks,)),
            dma((2, chunks)),
            dma((4,)),
            dma((2, group)),
            dma((2, group)),
            dma((2, group)),
            dma((layers, group)),
            dma((layers,)),
            dma((layers,)),
            dma((chunks, group)),
            dma((chunks, group)),
            dma((2, chunks, layers)),
            dma((chunks, layers)),
            dma((2, chips)),
            dma((2, chips)),
            dma((layers,)),
            dma((2,)),
            dma((peers,)),
            dma((2, chips)),
            dma((chunks, group)),
            dma((chunks, group)),
        ],
        compiler_params=pltpu.CompilerParams(collective_id=0, has_side_effects=True),
        name="stein",
    )(length_scale, models, gradients)
    return pl.pallas_call(
        functools.partial(expand_kernel, 1.0 / count),
        out_shape=jax.ShapeDtypeStruct(models.shape, jnp.float32),
        grid=(fields,),
        in_specs=[pl.BlockSpec((1, rows, width), lambda i: (i, 0, 0))],
        out_specs=pl.BlockSpec((1, rows, width), lambda i: (i, 0, 0)),
        name="expand",
    )(gathered)


def solution(mesh):
    spread, planes = mesh.shape["dom"], mesh.shape["cell"]
    layers = math.isqrt(spread)
    group = spread // layers

    def body(models, gradients, length_scale):
        _, rows, width = models.shape
        slab = group * rows
        chips = group // 2 * planes
        fits = (
            layers == 4
            and group == 4
            and models.shape[0] == 2
            and layers * group == spread
            and width % (group * 256) == 0
            and rows % 16 == 0
            and slab % 128 == 0
            and slab % (chips * 16) == 0
        )
        if not fits:
            return plain_body(models, gradients, length_scale)
        return fused_body(layers, group, planes, models, gradients, length_scale)

    placed = (P(None, "dom", "cell"), P(None, "dom", "cell"), P())
    return jax.shard_map(
        body, mesh=mesh, in_specs=placed, out_specs=P(None, "dom", "cell"), check_vma=False
    )
```
